512 devices in a mesh: seq: 64 (over z, y_lo, core), head: 8 (over y_hi, x).
Axes of the slice: x: 4, y: 8 (y_hi: 2, y_lo: 4; y = y_hi * 4 + y_lo), z: 8, core: 2. Of those that a mesh axis runs over, the one named last changes fastest.
Arguments:
- query_in: bfloat16 [24576, 2048], P('seq', 'head'), may hold values from -6 to 6
- key_in: bfloat16 [24576, 2048], P('seq', 'head'), may hold values from -6 to 6
- value_in: bfloat16 [24576, 2048], P('seq', 'head'), may hold values from -6 to 6
- text_keys: bfloat16 [256, 2048], P(None, 'head'), may hold values from -6 to 6
- text_values: bfloat16 [256, 2048], P(None, 'head'), may hold values from -6 to 6
- text_mask: int32 [256], replicated, may hold values 0 or 1
- window_reach: int32 [16, 2], P('head'), may hold values from 0 to 1
- tile_map: int32 [64, 3], replicated, may hold values from 0 to 14, as said below
- out_weight: bfloat16 [2048, 3072], P('head'), may hold values from -0.125 to 0.125
- gate_scale: float32 [3072], replicated, may hold values from -4 to 4
- grad_out: bfloat16 [24576, 3072], P('seq', 'head'), may hold values from -12 to 12
Outputs:
- grad_query: bfloat16 [24576, 2048], P('seq', 'head')
- grad_key: bfloat16 [24576, 2048], P('seq', 'head')
- grad_value: bfloat16 [24576, 2048], P('seq', 'head')
- grad_text_keys: bfloat16 [256, 2048], P(None, 'head')
- grad_text_values: bfloat16 [256, 2048], P(None, 'head')
- grad_gate: float32 [3072], replicated
The draws below stay inside these ranges and needn't reach their ends.
Inputs may be any that keep to these rules, and one draw needn't show every extreme that they name: `tile_map`: index i of seq sits at grid row i // 8 and grid column i % 8. Its tile row is that grid row, or 7 minus it, plus an offset; its tile column is the grid column, or 7 minus it, plus an offset; the mirroring and the offsets are the same for all indices, and so is the frame coordinate. Of the two offsets, the one of the longer grid dimension (rows when they are equal) is 7, the other 0.
All inputs are finite; a program needn't handle non-finite values.
Results may differ from the reference program's by a relative error of at most 0.02035.
The reference program's roundings to bfloat16 on the way (of `queries`, `rotated_keys`, `probs`, `attn`, `grad_proj`, `grad_attn` and `grad_scores`) count: a program that leaves them out, or rounds other values in their place, can miss the bound.
Values may be sent and summed in bfloat16 or wider, within the bound.
No kernel may reach another device: no remote copies, remote signals or barrier semaphores. Data moves between devices by JAX's collectives and lax.ppermute only.
A program may use at most 64 MiB of HBM per device.

```python
import jax
import jax.numpy as jnp
from jax import lax

D = 3072
HEAD_DIM = 128
HEADS = 16
TILE_T = 6
TILE_H = 8
TILE_W = 8
TILE = 384
COLS = 8
TXT = 256
TOKENS = 24576
N_SEQ = 64


def paired_draw(key):
    base = jax.random.fold_in(key, 7)
    first_key, second_key = jax.random.split(base, 2)
    token_total = N_SEQ * TILE_T * TILE_H * TILE_W
    feature_width = HEADS * HEAD_DIM
    queries = jnp.clip(1.5 * jax.random.normal(first_key, (token_total, feature_width), jnp.float32), -6.0, 6.0)
    keys_drawn = jnp.clip(1.5 * jax.random.normal(second_key, (token_total, feature_width), jnp.float32), -6.0, 6.0)
    return (queries, keys_drawn)


def draw_query_in(key, part):
    return paired_draw(key)[0].astype(jnp.bfloat16)


def draw_key_in(key, part):
    return paired_draw(key)[1].astype(jnp.bfloat16)


def draw_grad_out(key, part):
    base = jax.random.fold_in(key, 19)
    first_key = jax.random.fold_in(base, 0)
    token_total = N_SEQ * TILE_T * TILE_H * TILE_W
    noise = jnp.clip(jax.random.normal(first_key, (token_total, D), jnp.float32), -4.0, 4.0)
    ramp = jnp.arange(token_total, dtype=jnp.float32) / (token_total - 1)
    return (noise * (1.0 + 2.0 * ramp)[:, None]).astype(jnp.bfloat16)


def draw_tile_map(key, part):
    base = jax.random.fold_in(key, 31)
    flip_key, offset_key = jax.random.split(base)
    flips = jax.random.randint(flip_key, (2,), 0, 2)
    frame_offset = jax.random.randint(offset_key, (), 0, 5)
    device = jnp.arange(N_SEQ, dtype=jnp.int32)
    row_count = N_SEQ // COLS
    row_offset = 7 if row_count >= COLS else 0
    col_offset = 0 if row_count >= COLS else 7
    grid_row = device // COLS
    grid_col = device % COLS
    tile_row = jnp.where(flips[0] == 1, row_count - 1 - grid_row, grid_row) + row_offset
    tile_col = jnp.where(flips[1] == 1, COLS - 1 - grid_col, grid_col) + col_offset
    tile_frame = jnp.zeros_like(device) + frame_offset
    return jnp.stack([tile_frame, tile_row, tile_col], axis=1).astype(jnp.int32)


def place_ends(drawn, stream_key, smallest, top_value):
    dims = drawn.shape
    index_at = [jax.random.randint(jax.random.fold_in(stream_key, axis), (), 0, dims[axis]) for axis in range(len(dims))]
    drawn = drawn.at[tuple(index_at)].set(smallest)
    longest = dims.index(max(dims))
    index_at[longest] = (index_at[longest] + 1) % dims[longest]
    return drawn.at[tuple(index_at)].set(top_value)


def shard_levels(key, dims, shards, smallest, high):
    factor_of = 1.0
    for dim, parts in shards:
        steps = jax.random.uniform(jax.random.fold_in(jax.random.fold_in(key, 6), dim), (parts,), jnp.float32, smallest / len(shards), high / len(shards))
        factor_of = factor_of * jnp.repeat(jnp.exp(steps), dims[dim] // parts).reshape((-1,) + (1,) * (len(dims) - 1 - dim))
    return factor_of


def gaussian(key, extent, width, reach, cuts=(), kind=jnp.bfloat16):
    values = width * jax.random.normal(key, extent, jnp.float32)
    if cuts:
        values = values * shard_levels(key, extent, cuts, -0.22, 0.18)
    return jnp.clip(values, -reach, reach).astype(kind)


def setup_inputs(seed: int = 0) -> dict:
    seeds = jax.random.split(jax.random.key(seed), 12)
    query_in = draw_query_in(jax.random.fold_in(seeds[11], 71), 0)
    key_in = draw_key_in(jax.random.fold_in(seeds[11], 71), 0)
    value_in = gaussian(seeds[2], (TOKENS, HEADS * HEAD_DIM), 1.0, 6.0, ((0, 64), (1, 8)))
    text_keys = gaussian(seeds[3], (TXT, HEADS * HEAD_DIM), 1.5, 6.0, ((1, 8),))
    text_values = gaussian(seeds[4], (TXT, HEADS * HEAD_DIM), 1.0, 6.0, ((1, 8),))
    text_mask = place_ends((jax.random.randint(seeds[5], (TXT,), 0, 2) < 1).astype(jnp.int32), jax.random.fold_in(seeds[5], 1), 0, 1)
    window_reach = place_ends(jax.random.randint(seeds[6], (HEADS, 2), 0, 2), jax.random.fold_in(seeds[6], 1), 0, 1).astype(jnp.int32)
    tile_map = draw_tile_map(jax.random.fold_in(seeds[11], 71), 0)
    out_weight = gaussian(seeds[8], (HEADS * HEAD_DIM, D), (HEADS * HEAD_DIM) ** -0.5, 0.125, ((0, 8),))
    gate_scale = gaussian(seeds[9], (D,), 1.0, 4.0, (), jnp.float32)
    grad_out = draw_grad_out(jax.random.fold_in(seeds[11], 71), 0)
    return {"query_in": query_in, "key_in": key_in, "value_in": value_in, "text_keys": text_keys, "text_values": text_values, "text_mask": text_mask, "window_reach": window_reach, "tile_map": tile_map, "out_weight": out_weight, "gate_scale": gate_scale, "grad_out": grad_out}


theta_base = 256.0


def to_bf16(values):
    return lax.optimization_barrier(values.astype(jnp.bfloat16))


def sections(head_dim):
    first = head_dim // 8
    second = (head_dim - first) // 2
    return ((0, first), (first, second), (first + second, second))


def rotate(values, frame_pos, row_pos, col_pos, direction):
    pieces = []
    for (offset, length), where_pos in zip(sections(values.shape[-1]), (frame_pos, row_pos, col_pos)):
        half_len = length // 2
        freqs = theta_base ** (-2.0 * jnp.arange(half_len, dtype=jnp.float32) / length)
        angles = where_pos.astype(jnp.float32)[:, None] * freqs[None, :]
        cosine = jnp.cos(angles)[:, None, :]
        sine_part = jnp.sin(angles)[:, None, :]
        first_half = values[..., offset:offset + half_len]
        second_half = values[..., offset + half_len:offset + length]
        pieces.append(first_half * cosine - direction * second_half * sine_part)
        pieces.append(direction * first_half * sine_part + second_half * cosine)
    return jnp.concatenate(pieces, axis=-1)


def local_positions(tile_coords):
    local_index = jnp.arange(TILE_T * TILE_H * TILE_W, dtype=jnp.int32)
    plane_size = TILE_H * TILE_W
    frame_pos = tile_coords[:, 0:1] * TILE_T + (local_index // plane_size)[None, :]
    row_pos = tile_coords[:, 1:2] * TILE_H + ((local_index // TILE_W) % TILE_H)[None, :]
    col_pos = tile_coords[:, 2:3] * TILE_W + (local_index % TILE_W)[None, :]
    return frame_pos.reshape(-1), row_pos.reshape(-1), col_pos.reshape(-1)


def reference(query_in, key_in, value_in, text_keys, text_values, text_mask, window_reach, tile_map, out_weight, gate_scale, grad_out):
    score_scale = HEAD_DIM ** -0.5
    head_shape = (TOKENS, HEADS, HEAD_DIM)
    tile_shape = (N_SEQ, TILE, HEADS, HEAD_DIM)
    frame_pos, row_pos, col_pos = local_positions(tile_map)
    queries = to_bf16(rotate(query_in.astype(jnp.float32).reshape(head_shape), frame_pos, row_pos, col_pos, 1.0))
    rotated_keys = to_bf16(rotate(key_in.astype(jnp.float32).reshape(head_shape), frame_pos, row_pos, col_pos, 1.0))
    queries_t = queries.reshape(tile_shape)
    keys_t = rotated_keys.reshape(tile_shape)
    values_t = value_in.reshape(tile_shape)

    row_count = N_SEQ // COLS
    row_rel = tile_map[:, 1] - jnp.min(tile_map[:, 1])
    col_rel = tile_map[:, 2] - jnp.min(tile_map[:, 2])
    lookup = jnp.zeros((row_count, COLS), jnp.int32).at[row_rel, col_rel].set(jnp.arange(N_SEQ, dtype=jnp.int32))
    row_steps = jnp.array([-1, -1, -1, 0, 0, 0, 1, 1, 1], jnp.int32)
    col_steps = jnp.array([-1, 0, 1, -1, 0, 1, -1, 0, 1], jnp.int32)
    near_row = row_rel[:, None] + row_steps[None, :]
    near_col = col_rel[:, None] + col_steps[None, :]
    usable = (near_row >= 0) & (near_row < row_count) & (near_col >= 0) & (near_col < COLS)
    near = lookup[jnp.clip(near_row, 0, row_count - 1), jnp.clip(near_col, 0, COLS - 1)]
    allowed = usable[:, :, None] & (jnp.abs(row_steps)[None, :, None] <= window_reach[None, None, :, 0]) & (jnp.abs(col_steps)[None, :, None] <= window_reach[None, None, :, 1])

    text_open = text_mask == 1
    text_keys_f = text_keys.astype(jnp.float32).reshape(TXT, HEADS, HEAD_DIM)
    text_values_f = text_values.astype(jnp.float32).reshape(TXT, HEADS, HEAD_DIM)
    video_keys = 9 * TILE

    def key_set(index):
        near_keys = keys_t[near[index]].astype(jnp.float32).reshape(video_keys, HEADS, HEAD_DIM)
        near_values = values_t[near[index]].astype(jnp.float32).reshape(video_keys, HEADS, HEAD_DIM)
        all_keys = jnp.concatenate([near_keys, text_keys_f], axis=0)
        all_values = jnp.concatenate([near_values, text_values_f], axis=0)
        block_mask = jnp.repeat(allowed[index].T, TILE, axis=1)
        full_mask = jnp.concatenate([block_mask, jnp.broadcast_to(text_open[None, :], (HEADS, TXT))], axis=1)
        return all_keys, all_values, full_mask

    def forward_tile(index):
        all_keys, all_values, full_mask = key_set(index)
        query_f = queries_t[index].astype(jnp.float32)
        scores = jnp.einsum("qhd,khd->hqk", query_f, all_keys) * score_scale
        scores = jnp.where(full_mask[:, None, :], scores, -jnp.inf)
        peak = jnp.max(scores, axis=-1)
        log_norm = peak + jnp.log(jnp.sum(jnp.exp(scores - peak[..., None]), axis=-1))
        weights = jnp.where(full_mask[:, None, :], jnp.exp(scores - log_norm[..., None]), 0.0)
        probs = to_bf16(weights).astype(jnp.float32)
        attn = to_bf16(jnp.einsum("hqk,khd->qhd", probs, all_values))
        return log_norm, attn

    log_norms, attn = lax.map(forward_tile, jnp.arange(N_SEQ, dtype=jnp.int32))
    attn_flat = attn.reshape(TOKENS, HEADS * HEAD_DIM)
    grad_proj = to_bf16(grad_out.astype(jnp.float32) * gate_scale[None, :])
    grad_attn = to_bf16(jnp.dot(grad_proj, out_weight.T, preferred_element_type=jnp.float32))
    projected = jnp.dot(attn_flat, out_weight, preferred_element_type=jnp.float32)
    grad_gate = jnp.sum(grad_out.astype(jnp.float32) * projected, axis=0)
    grad_t = grad_attn.reshape(tile_shape)
    deltas = jnp.einsum("nqhd,nqhd->nhq", grad_t.astype(jnp.float32), attn.astype(jnp.float32))

    def query_tile(index):
        all_keys, all_values, full_mask = key_set(index)
        query_f = queries_t[index].astype(jnp.float32)
        grad_f = grad_t[index].astype(jnp.float32)
        scores = jnp.einsum("qhd,khd->hqk", query_f, all_keys) * score_scale
        weights = jnp.where(full_mask[:, None, :], jnp.exp(scores - log_norms[index][..., None]), 0.0)
        grad_weights = jnp.einsum("qhd,khd->hqk", grad_f, all_values)
        grad_scores = to_bf16(weights * (grad_weights - deltas[index][..., None])).astype(jnp.float32)
        grad_q = jnp.einsum("hqk,khd->qhd", grad_scores, all_keys) * score_scale
        text_key_part = jnp.einsum("hqk,qhd->khd", grad_scores[:, :, video_keys:], query_f) * score_scale
        text_probs = to_bf16(weights[:, :, video_keys:]).astype(jnp.float32)
        text_value_part = jnp.einsum("hqk,qhd->khd", text_probs, grad_f)
        return grad_q, text_key_part, text_value_part

    grad_qs, text_key_parts, text_value_parts = lax.map(query_tile, jnp.arange(N_SEQ, dtype=jnp.int32))

    def key_tile(index):
        near_index = near[index]
        query_f = queries_t[near_index].astype(jnp.float32).reshape(video_keys, HEADS, HEAD_DIM)
        grad_f = grad_t[near_index].astype(jnp.float32).reshape(video_keys, HEADS, HEAD_DIM)
        norms_near = log_norms[near_index].transpose(1, 0, 2).reshape(HEADS, video_keys)
        deltas_near = deltas[near_index].transpose(1, 0, 2).reshape(HEADS, video_keys)
        block_mask = jnp.repeat(allowed[index].T, TILE, axis=1)
        key_f = keys_t[index].astype(jnp.float32)
        value_f = values_t[index].astype(jnp.float32)
        scores = jnp.einsum("qhd,khd->hqk", query_f, key_f) * score_scale
        weights = jnp.where(block_mask[:, :, None], jnp.exp(scores - norms_near[:, :, None]), 0.0)
        grad_weights = jnp.einsum("qhd,khd->hqk", grad_f, value_f)
        grad_scores = to_bf16(weights * (grad_weights - deltas_near[:, :, None])).astype(jnp.float32)
        key_part = jnp.einsum("hqk,qhd->khd", grad_scores, query_f) * score_scale
        value_part = jnp.einsum("hqk,qhd->khd", to_bf16(weights).astype(jnp.float32), grad_f)
        return key_part, value_part

    key_parts, value_parts = lax.map(key_tile, jnp.arange(N_SEQ, dtype=jnp.int32))
    flat_width = HEADS * HEAD_DIM
    grad_query = rotate(grad_qs.reshape(head_shape), frame_pos, row_pos, col_pos, -1.0).astype(jnp.bfloat16).reshape(TOKENS, flat_width)
    grad_key = rotate(key_parts.reshape(head_shape), frame_pos, row_pos, col_pos, -1.0).astype(jnp.bfloat16).reshape(TOKENS, flat_width)
    grad_value = value_parts.reshape(TOKENS, flat_width).astype(jnp.bfloat16)
    grad_text_keys = jnp.sum(text_key_parts, axis=0).reshape(TXT, flat_width).astype(jnp.bfloat16)
    grad_text_values = jnp.sum(text_value_parts, axis=0).reshape(TXT, flat_width).astype(jnp.bfloat16)
    return grad_query, grad_key, grad_value, grad_text_keys, grad_text_values, grad_gate
```

```python
import functools
import math

import jax
import jax.numpy as jnp
import numpy as np
from jax import lax
from jax.experimental import pallas as pl
from jax.experimental.pallas import tpu as pltpu
from jax.sharding import Mesh
from jax.sharding import PartitionSpec as P


HEAD_DIM = 128
TILE_H = 8
TILE_W = 8
SECTIONS = ((0, 16), (16, 56), (72, 56))
THETA = 256.0
SCALE = HEAD_DIM ** -0.5
LOG2E = math.log2(math.e)
C1 = SCALE * LOG2E
SEQ = ("z", "y", "core")
COL = ("y", "core")
HEAD = ("yhi", "x")
F32 = jnp.float32
BF16 = jnp.bfloat16
NEG = -1e30
VMEM_LIMIT = 40 * 1024 * 1024
OFFSETS = tuple((a, b) for a in (-1, 0, 1) for b in (-1, 0, 1))


def dot_nn(a, b):
    return lax.dot_general(a, b, (((1,), (0,)), ((), ())), preferred_element_type=F32)


def dot_nt(a, b):
    return lax.dot_general(a, b, (((1,), (1,)), ((), ())), preferred_element_type=F32)


def dot_tn(a, b):
    return lax.dot_general(a, b, (((0,), (0,)), ((), ())), preferred_element_type=F32)


def params(*semantics):
    return pltpu.CompilerParams(
        dimension_semantics=semantics or None, vmem_limit_bytes=VMEM_LIMIT
    )


def lane_freqs():
    freqs = np.zeros((8, HEAD_DIM), np.float32)
    for offset, length in SECTIONS:
        half = length // 2
        f = np.float32(THETA) ** (
            np.float32(-2.0) * np.arange(half, dtype=np.float32) / np.float32(length)
        )
        freqs[:, offset : offset + half] = f
        freqs[:, offset + half : offset + length] = f
    return freqs


def partner(x, lane):
    near = jnp.where(lane < 8, pltpu.roll(x, HEAD_DIM - 8, 1), pltpu.roll(x, 8, 1))
    first = ((lane >= 16) & (lane < 44)) | ((lane >= 72) & (lane < 100))
    far = jnp.where(first, pltpu.roll(x, HEAD_DIM - 28, 1), pltpu.roll(x, 28, 1))
    return jnp.where(lane < 16, near, far)


def whole(shape):
    return pl.BlockSpec(shape, lambda *_: (0,) * len(shape))


def smem():
    return pl.BlockSpec(memory_space=pltpu.SMEM)


def rot_kernel(info, freq, q, k, v, q_out, kv_out, cos_out, sin_out):
    tile = q.shape[0]

    @pl.when(pl.program_id(0) == 0)
    def _():
        frames = tile // (TILE_H * TILE_W)
        step = lax.broadcasted_iota(jnp.int32, (8, HEAD_DIM), 0)
        lane = lax.broadcasted_iota(jnp.int32, (8, HEAD_DIM), 1)
        first = (
            (lane < 8) | ((lane >= 16) & (lane < 44)) | ((lane >= 72) & (lane < 100))
        )
        f = freq[...]

        def table(base):
            angle = (base + step).astype(F32) * f
            s = jnp.sin(angle)
            return jnp.cos(angle), jnp.where(first, -s, s)

        cf, sf = table(info[4] * frames)
        cr, sr = table(info[5] * TILE_H)
        cc, sc = table(info[6] * TILE_W)
        for r in range(TILE_H):
            crr = jnp.where(lane < 72, cr[r : r + 1, :], cc)
            srr = jnp.where(lane < 72, sr[r : r + 1, :], sc)
            for t in range(frames):
                at = (t * TILE_H + r) * TILE_W
                cos_out[at : at + TILE_W, :] = jnp.where(lane < 16, cf[t : t + 1, :], crr)
                sin_out[at : at + TILE_W, :] = jnp.where(lane < 16, sf[t : t + 1, :], srr)

    lane = lax.broadcasted_iota(jnp.int32, (tile, HEAD_DIM), 1)
    cos, sin = cos_out[...], sin_out[...]
    for source, target in ((q, q_out), (k, kv_out.at[0])):
        x = source[...].astype(F32)
        target[...] = (x * cos + partner(x, lane) * sin).astype(BF16)
    kv_out[1] = v[...]


def rotate_call(info, q_in, k_in, v_in):
    tile, width = q_in.shape
    heads = width // HEAD_DIM
    half = pl.BlockSpec((tile, HEAD_DIM), lambda h: (0, h))
    table = whole((tile, HEAD_DIM))
    return pl.pallas_call(
        rot_kernel,
        grid=(heads,),
        in_specs=[smem(), whole((8, HEAD_DIM)), half, half, half],
        out_specs=[half, pl.BlockSpec((2, tile, HEAD_DIM), lambda h: (0, 0, h)), table, table],
        out_shape=[
            jax.ShapeDtypeStruct((tile, width), BF16),
            jax.ShapeDtypeStruct((2, tile, width), BF16),
            jax.ShapeDtypeStruct((tile, HEAD_DIM), F32),
            jax.ShapeDtypeStruct((tile, HEAD_DIM), F32),
        ],
        compiler_params=params("arbitrary"),
        name="rot",
    )(info, jnp.asarray(lane_freqs()), q_in, k_in, v_in)


def open_block(info, h, a, b):
    ok = (info[8 + 2 * h] >= abs(a)) & (info[9 + 2 * h] >= abs(b))
    if a:
        row = info[0] + a
        ok = ok & (row >= 0) & (row < info[2])
    if b:
        col = info[1] + b
        ok = ok & (col >= 0) & (col < info[3])
    return ok


def fwd_kernel(info, q, *refs):
    blocks, (tk, tv, bias, ot_out, lse_out, m, l, acc) = refs[:9], refs[9:]
    h = pl.program_id(0)
    m[...] = jnp.full(m.shape, NEG, F32)
    l[...] = jnp.zeros(l.shape, F32)
    acc[...] = jnp.zeros(acc.shape, F32)

    def block(keys, values, extra):
        s = dot_nt(keys, q[...]) * C1
        if extra is not None:
            s = s + extra
        m_old = m[0:1, :]
        m_new = jnp.maximum(m_old, jnp.max(s, axis=0, keepdims=True))
        p = jnp.exp2(s - m_new)
        alpha = jnp.exp2(m_old - m_new)
        m[0:1, :] = m_new
        l[0:1, :] = l[0:1, :] * alpha + jnp.sum(p, axis=0, keepdims=True)
        acc[...] = acc[...] * alpha + dot_tn(values, p.astype(BF16))

    order = [4] + [i for i in range(9) if i != 4]
    for i in order:
        a, b = OFFSETS[i]
        if i == 4:
            block(blocks[i][0], blocks[i][1], None)
            block(tk[...], tv[...], bias[...])
        else:

            @pl.when(open_block(info, h, a, b))
            def _(i=i):
                block(blocks[i][0], blocks[i][1], None)

    ot_out[...] = (acc[...] * (1.0 / l[0:1, :])).astype(BF16)
    lse_out[...] = jnp.broadcast_to(m[0:1, :] + jnp.log2(l[0:1, :]), lse_out.shape)


def kv_spec(tile):
    return pl.BlockSpec((2, tile, HEAD_DIM), lambda h: (0, 0, h))


def forward_call(info, q, blocks, text_keys, text_values, bias):
    tile, width = q.shape
    heads = width // HEAD_DIM
    txt = text_keys.shape[0]
    half = pl.BlockSpec((tile, HEAD_DIM), lambda h: (0, h))
    thalf = pl.BlockSpec((txt, HEAD_DIM), lambda h: (0, h))
    keys = 9 * tile + txt
    return pl.pallas_call(
        fwd_kernel,
        grid=(heads,),
        in_specs=[smem(), half] + [kv_spec(tile)] * 9 + [thalf, thalf, whole((txt, 1))],
        out_specs=[
            pl.BlockSpec((HEAD_DIM, tile), lambda h: (h, 0)),
            pl.BlockSpec((8, tile), lambda h: (h, 0)),
        ],
        out_shape=[
            jax.ShapeDtypeStruct((width, tile), BF16),
            jax.ShapeDtypeStruct((8 * heads, tile), F32),
        ],
        scratch_shapes=[
            pltpu.VMEM((8, tile), F32),
            pltpu.VMEM((8, tile), F32),
            pltpu.VMEM((HEAD_DIM, tile), F32),
        ],
        compiler_params=params("arbitrary"),
        cost_estimate=pl.CostEstimate(
            flops=4 * tile * keys * width, bytes_accessed=4 * keys * width, transcendentals=0
        ),
        name="fwd",
    )(info, q, *blocks, text_keys, text_values, bias)


def proj_kernel(steps, last, info, w, gate, ot, *refs):
    pieces, rest = refs[: len(steps)], refs[len(steps) :]
    if last:
        acc_in, gate_in, dot_out, delta_out, gate_out = rest
    else:
        acc_out, gate_out = rest
    heads_x, heads_y = info[16], info[17]
    acc = acc_in[...] if last else None
    if last:
        gate_out[...] = gate_in[...]
    else:
        gate_out[...] = jnp.zeros(gate_out.shape, F32)
    tile = ot.shape[1]
    for piece, (flip, dx) in zip(pieces, steps):
        y = info[18] if not flip else heads_y - 1 - info[18]
        x = lax.rem(info[19] + dx + heads_x, heads_x)
        block = y * heads_x + x
        cols = piece.shape[1]
        at = pl.multiple_of(block * cols, 128)
        g = piece[...].astype(F32)
        scaled = (g * gate[:, pl.ds(at, cols)]).astype(BF16)
        wp = w[:, pl.ds(at, cols)]
        part = dot_nt(wp, scaled)
        acc = part if acc is None else acc + part
        terms = dot_nn(ot[...], piece[...]) * wp.astype(F32)
        row = jnp.sum(terms, axis=0, keepdims=True)
        for i in range(cols // 128):
            gate_out[pl.ds(block * (cols // 128) + i, 1), :] = row[:, i * 128 : (i + 1) * 128]
    if not last:
        acc_out[...] = acc
    else:
        rounded = acc.astype(BF16)
        dot_out[...] = rounded
        prod = rounded.astype(F32) * ot[...].astype(F32)
        for h in range(ot.shape[0] // HEAD_DIM):
            d = jnp.sum(prod[h * HEAD_DIM : (h + 1) * HEAD_DIM, :], axis=0, keepdims=True)
            delta_out[8 * h : 8 * h + 8, :] = jnp.broadcast_to(d, (8, tile))


def proj_call(steps, info, w, gate, ot, pieces, carried=None):
    width, tile = ot.shape
    heads = width // HEAD_DIM
    cols = pieces[0].shape[1]
    rows = w.shape[1] // 128
    last = carried is not None
    acc = jax.ShapeDtypeStruct((width, tile), F32)
    gates = jax.ShapeDtypeStruct((rows, 128), F32)
    if last:
        out_shape = [
            jax.ShapeDtypeStruct((width, tile), BF16),
            jax.ShapeDtypeStruct((8 * heads, tile), F32),
            gates,
        ]
    else:
        out_shape = [acc, gates]
    operands = (info, w, gate, ot, *pieces) + (tuple(carried) if last else ())
    return pl.pallas_call(
        functools.partial(proj_kernel, steps, last),
        in_specs=[smem()] + [pl.BlockSpec(memory_space=pltpu.VMEM)] * (len(operands) - 1),
        out_specs=[pl.BlockSpec(memory_space=pltpu.VMEM)] * len(out_shape),
        out_shape=out_shape,
        compiler_params=params(),
        cost_estimate=pl.CostEstimate(
            flops=4 * tile * width * cols * len(pieces),
            bytes_accessed=2 * tile * cols * len(pieces) + 2 * w.size,
            transcendentals=0,
        ),
        name="proj",
    )(*operands)


def bwd_math(keys, values, q, dot, lse, delta, dq, extra):
    s = dot_nt(keys, q[...]) * C1
    if extra is not None:
        s = s + extra
    p = jnp.exp2(s - lse[0:1, :])
    dp = dot_nn(values, dot[...])
    ds = (p * (dp - delta[0:1, :])).astype(BF16)
    dv = dot_nt(p.astype(BF16), dot[...])
    dk = dot_nn(ds, q[...]) * SCALE
    dq[...] += dot_tn(keys, ds)
    return dk, dv


def bwd_blocks(info, h, offsets, blocks, outs, q, dot, lse, delta, dq):
    for (a, b), block, out in zip(offsets, blocks, outs):

        def run(block=block, out=out):
            dk, dv = bwd_math(block[0], block[1], q, dot, lse, delta, dq, None)
            out[0] = dk.astype(out.dtype)
            out[1] = dv.astype(out.dtype)

        if (a, b) == (0, 0):
            run()
        else:
            ok = open_block(info, h, a, b)
            pl.when(ok)(run)

            @pl.when(jnp.logical_not(ok))
            def _(out=out):
                out[...] = jnp.zeros(out.shape, out.dtype)


def bwd_first_kernel(offsets, info, q, dot, lse, delta, tk, tv, bias, *refs):
    n = len(offsets)
    blocks, outs, (text_out, dq_out) = refs[:n], refs[n : 2 * n], refs[2 * n :]
    h = pl.program_id(0)
    dq_out[...] = jnp.zeros(dq_out.shape, F32)
    dk, dv = bwd_math(tk[...], tv[...], q, dot, lse, delta, dq_out, bias[...])
    text_out[0] = dk.astype(BF16)
    text_out[1] = dv.astype(BF16)
    bwd_blocks(info, h, offsets, blocks, outs, q, dot, lse, delta, dq_out)


def bwd_last_kernel(offsets, info, q, dot, lse, delta, dq_in, cos, sin, *refs):
    n = len(offsets)
    blocks, outs, (gq_out, dq) = refs[:n], refs[n : 2 * n], refs[2 * n :]
    h = pl.program_id(0)
    dq[...] = dq_in[...]
    bwd_blocks(info, h, offsets, blocks, outs, q, dot, lse, delta, dq)
    x = jnp.transpose(dq[...]) * SCALE
    lane = lax.broadcasted_iota(jnp.int32, x.shape, 1)
    gq_out[...] = (x * cos[...] - partner(x, lane) * sin[...]).astype(BF16)


def bwd_specs(tile):
    return [
        smem(),
        pl.BlockSpec((tile, HEAD_DIM), lambda h: (0, h)),
        pl.BlockSpec((HEAD_DIM, tile), lambda h: (h, 0)),
        pl.BlockSpec((8, tile), lambda h: (h, 0)),
        pl.BlockSpec((8, tile), lambda h: (h, 0)),
    ]


def bwd_cost(tile, keys, width):
    return pl.CostEstimate(
        flops=10 * tile * keys * width, bytes_accessed=8 * keys * width, transcendentals=0
    )


def bwd_first_call(offsets, common, text_keys, text_values, bias, blocks):
    info, q, dot, lse, delta = common
    tile, width = q.shape
    txt = text_keys.shape[0]
    n = len(offsets)
    thalf = pl.BlockSpec((txt, HEAD_DIM), lambda h: (0, h))
    return pl.pallas_call(
        functools.partial(bwd_first_kernel, offsets),
        grid=(width // HEAD_DIM,),
        in_specs=bwd_specs(tile) + [thalf, thalf, whole((txt, 1))] + [kv_spec(tile)] * n,
        out_specs=[kv_spec(tile)] * n
        + [kv_spec(txt), pl.BlockSpec((HEAD_DIM, tile), lambda h: (h, 0))],
        out_shape=[jax.ShapeDtypeStruct((2, tile, width), BF16)] * n
        + [
            jax.ShapeDtypeStruct((2, txt, width), BF16),
            jax.ShapeDtypeStruct((width, tile), F32),
        ],
        compiler_params=params("arbitrary"),
        cost_estimate=bwd_cost(tile, n * tile + txt, width),
        name="bwd_first",
    )(info, q, dot, lse, delta, text_keys, text_values, bias, *blocks)


def bwd_last_call(offsets, kinds, common, dq, cos, sin, blocks):
    info, q, dot, lse, delta = common
    tile, width = q.shape
    n = len(offsets)
    table = whole((tile, HEAD_DIM))
    return pl.pallas_call(
        functools.partial(bwd_last_kernel, offsets),
        grid=(width // HEAD_DIM,),
        in_specs=bwd_specs(tile)
        + [pl.BlockSpec((HEAD_DIM, tile), lambda h: (h, 0)), table, table]
        + [kv_spec(tile)] * n,
        out_specs=[kv_spec(tile)] * n + [pl.BlockSpec((tile, HEAD_DIM), lambda h: (0, h))],
        out_shape=[jax.ShapeDtypeStruct((2, tile, width), kind) for kind in kinds]
        + [jax.ShapeDtypeStruct((tile, width), BF16)],
        scratch_shapes=[pltpu.VMEM((HEAD_DIM, tile), F32)],
        compiler_params=params("arbitrary"),
        cost_estimate=bwd_cost(tile, n * tile, width),
        name="bwd_last",
    )(info, q, dot, lse, delta, dq, cos, sin, *blocks)


def pair_sum_kernel(up, up_l, up_r, dn, dn_l, dn_r, up_out, dn_out):
    up_out[...] = (up[...] + up_l[...].astype(F32) + up_r[...].astype(F32)).astype(BF16)
    dn_out[...] = (dn[...] + dn_l[...].astype(F32) + dn_r[...].astype(F32)).astype(BF16)


def pair_sum_call(*operands):
    tile, width = operands[0].shape[1:]
    spec = kv_spec(tile)
    shape = jax.ShapeDtypeStruct((2, tile, width), BF16)
    return pl.pallas_call(
        pair_sum_kernel,
        grid=(width // HEAD_DIM,),
        in_specs=[spec] * 6,
        out_specs=[spec] * 2,
        out_shape=[shape] * 2,
        compiler_params=params("arbitrary"),
        name="pair_sum",
    )(*operands)


def finish_kernel(own, left, right, up, dn, cos, sin, gk_out, gv_out):
    total = own[...]
    for other in (left, right, up, dn):
        total = total + other[...].astype(F32)
    x = total[0]
    lane = lax.broadcasted_iota(jnp.int32, x.shape, 1)
    gk_out[...] = (x * cos[...] - partner(x, lane) * sin[...]).astype(BF16)
    gv_out[...] = total[1].astype(BF16)


def finish_call(own, left, right, up, dn, cos, sin):
    tile, width = own.shape[1:]
    half = pl.BlockSpec((tile, HEAD_DIM), lambda h: (0, h))
    table = whole((tile, HEAD_DIM))
    shape = jax.ShapeDtypeStruct((tile, width), BF16)
    return pl.pallas_call(
        finish_kernel,
        grid=(width // HEAD_DIM,),
        in_specs=[kv_spec(tile)] * 5 + [table, table],
        out_specs=[half, half],
        out_shape=[shape, shape],
        compiler_params=params("arbitrary"),
        name="finish",
    )(own, left, right, up, dn, cos, sin)


def pack_kernel(text, gate, out):
    groups = out.shape[0]
    rows, width = out.shape[1], text.shape[1]
    out[:, :, :width] = text[...].reshape(groups, rows, width)
    out[:, :, width:] = jnp.zeros((groups, rows, 128), BF16)
    for i in range(gate.shape[0]):
        hi = gate[i : i + 1, :].astype(BF16)
        out[i, 0:1, width:] = hi
        out[i, 1:2, width:] = (gate[i : i + 1, :] - hi.astype(F32)).astype(BF16)


def pack_call(text, gate, groups):
    rows = text.shape[0] // groups
    return pl.pallas_call(
        pack_kernel,
        in_specs=[pl.BlockSpec(memory_space=pltpu.VMEM)] * 2,
        out_specs=pl.BlockSpec(memory_space=pltpu.VMEM),
        out_shape=jax.ShapeDtypeStruct((groups, rows, text.shape[1] + 128), BF16),
        compiler_params=params(),
        name="pack",
    )(text, gate)


def chunk_sum_kernel(width, got, out):
    total = jnp.sum(got[...].astype(F32), axis=0)
    text = total[:, :width].astype(BF16)
    gate = total[0:1, width:] + total[1:2, width:]
    hi = gate.astype(BF16)
    lo = (gate - hi.astype(F32)).astype(BF16)
    row = lax.broadcasted_iota(jnp.int32, (total.shape[0], 128), 0)
    side = jnp.where(
        row == 0, hi.astype(F32), jnp.where(row == 1, lo.astype(F32), 0.0)
    ).astype(BF16)
    groups = out.shape[0]
    out[:, :, :width] = jnp.broadcast_to(text[None], (groups, *text.shape))
    out[:, :, width:] = jnp.broadcast_to(side[None], (groups, *side.shape))


def chunk_sum_call(got, width):
    return pl.pallas_call(
        functools.partial(chunk_sum_kernel, width),
        in_specs=[pl.BlockSpec(memory_space=pltpu.VMEM)],
        out_specs=pl.BlockSpec(memory_space=pltpu.VMEM),
        out_shape=jax.ShapeDtypeStruct(got.shape, BF16),
        compiler_params=params(),
        name="chunk_sum",
    )(got)


def unpack_kernel(width, got, keys_out, values_out, gate_out):
    groups, rows, _ = got.shape
    half = groups // 2
    keys_out[...] = got[:half, :, :width].reshape(half * rows, width)
    values_out[...] = got[half:, :, :width].reshape(half * rows, width)
    for i in range(gate_out.shape[0]):
        pair = got[i, :, width:].astype(F32)
        gate_out[i : i + 1, :] = pair[0:1, :] + pair[1:2, :]


def unpack_call(got, width, gate_rows):
    groups, rows, _ = got.shape
    text = jax.ShapeDtypeStruct((groups // 2 * rows, width), BF16)
    return pl.pallas_call(
        functools.partial(unpack_kernel, width),
        in_specs=[pl.BlockSpec(memory_space=pltpu.VMEM)],
        out_specs=[pl.BlockSpec(memory_space=pltpu.VMEM)] * 3,
        out_shape=[text, text, jax.ShapeDtypeStruct((gate_rows, 128), F32)],
        compiler_params=params(),
        name="unpack",
    )(got)


def shift(array, axis, by, wrap=False):
    length = lax.axis_size(axis)
    pairs = [(i, (i + by) % length) for i in range(length) if wrap or 0 <= i + by < length]
    return lax.ppermute(array, axis, pairs)


def swap(array, axis, bit):
    length = lax.axis_size(axis)
    return lax.ppermute(array, axis, [(i, i ^ bit) for i in range(length)])


def on_device(
    query_in,
    key_in,
    value_in,
    text_keys,
    text_values,
    text_mask,
    window_reach,
    tile_map,
    out_weight,
    gate_scale,
    grad_out,
):
    tile, width = query_in.shape
    seq_count = lax.axis_size(SEQ)
    row, col = lax.axis_index("z"), lax.axis_index(COL)
    coords = lax.dynamic_slice(tile_map, (lax.axis_index(SEQ), 0), (1, 3))[0]
    counts = jnp.array(
        [lax.axis_size("z"), lax.axis_size(COL)], jnp.int32
    )
    info = jnp.concatenate(
        [
            jnp.stack([row, col]).astype(jnp.int32),
            counts,
            coords,
            jnp.zeros((1,), jnp.int32),
            window_reach.reshape(-1),
            jnp.zeros((8 - window_reach.size,), jnp.int32),
            jnp.array([lax.axis_size("x"), lax.axis_size("yhi")], jnp.int32),
            jnp.stack([lax.axis_index("yhi"), lax.axis_index("x")]).astype(jnp.int32),
        ]
    )
    bias = jnp.where(text_mask == 1, 0.0, NEG).astype(F32)[:, None]

    half = tile // 2
    g_y = swap(grad_out, "yhi", 1)
    g_r = shift(grad_out, "x", 1, True)
    g_l = shift(grad_out, "x", -1, True)

    q, kv, cos, sin = rotate_call(info, query_in, key_in, value_in)

    block = {(0, 0): kv, (-1, 0): shift(kv, "z", 1), (1, 0): shift(kv, "z", -1)}
    for a in (0, -1, 1):
        block[a, -1] = shift(block[a, 0], COL, 1)
        block[a, 1] = shift(block[a, 0], COL, -1)

    def far(from_left, from_right):
        top = shift(from_left[:half], "x", 1, True)
        bottom = shift(from_right[half:], "x", -1, True)
        return jnp.concatenate([top, bottom], axis=0)

    g_far = far(g_r, g_l)
    gy_r = shift(g_y, "x", 1, True)
    gy_l = shift(g_y, "x", -1, True)
    gy_far = far(gy_r, gy_l)

    ot, lse = forward_call(
        info, q, [block[o] for o in OFFSETS], text_keys, text_values, bias
    )

    gate = gate_scale.reshape(1, -1)
    steps = ((False, 0), (False, -1), (False, 1), (False, 2))
    carried = proj_call(steps, info, out_weight, gate, ot, [grad_out, g_r, g_l, g_far])
    steps = ((True, 0), (True, -1), (True, 1), (True, 2))
    dot, delta, gate_terms = proj_call(
        steps, info, out_weight, gate, ot, [g_y, gy_r, gy_l, gy_far], carried
    )
    for axis, bits in (("x", lax.axis_size("x")), ("yhi", lax.axis_size("yhi"))):
        bit = 1
        while bit < bits:
            gate_terms = gate_terms + swap(gate_terms, axis, bit)
            bit *= 2

    common = (info, q, dot, lse, delta)
    corners = ((-1, -1), (-1, 1), (1, -1), (1, 1))
    *parts, text_part, dq = bwd_first_call(
        corners, common, text_keys, text_values, bias, [block[o] for o in corners]
    )
    back = {}
    for (a, b), part in zip(corners, parts):
        back[a, b] = shift(part, COL, b)
    rest = ((0, -1), (0, 1), (-1, 0), (1, 0), (0, 0))
    left, right, up, down, own, grad_query = bwd_last_call(
        rest, (BF16, BF16, F32, F32, F32), common, dq, cos, sin, [block[o] for o in rest]
    )
    back[0, -1] = shift(left, COL, -1)
    back[0, 1] = shift(right, COL, 1)

    packed = pack_call(text_part.reshape(-1, width), gate_terms, seq_count)
    got = lax.all_to_all(packed, SEQ, 0, 0, tiled=True)

    up, down = pair_sum_call(
        up, back[-1, -1], back[-1, 1], down, back[1, -1], back[1, 1]
    )
    up = shift(up, "z", -1)
    down = shift(down, "z", 1)

    summed = lax.all_to_all(chunk_sum_call(got, width), SEQ, 0, 0, tiled=True)
    grad_text_keys, grad_text_values, grad_gate = unpack_call(
        summed, width, out_weight.shape[1] // 128
    )
    grad_key, grad_value = finish_call(own, back[0, -1], back[0, 1], up, down, cos, sin)
    return (
        grad_query,
        grad_key,
        grad_value,
        grad_text_keys,
        grad_text_values,
        grad_gate.reshape(-1),
    )


def solution(mesh):
    sizes = FINE_SIZES if FINE_SIZES is not None else (8, 4, 2, 2, 4)
    fine = Mesh(mesh.devices.reshape(sizes), (*SEQ, *HEAD))
    placed = (
        P(SEQ, HEAD),
        P(SEQ, HEAD),
        P(SEQ, HEAD),
        P(None, HEAD),
        P(None, HEAD),
        P(),
        P(HEAD, None),
        P(),
        P(HEAD, None),
        P(),
        P(SEQ, HEAD),
    )
    return jax.shard_map(
        on_device,
        mesh=fine,
        in_specs=placed,
        out_specs=(
            P(SEQ, HEAD),
            P(SEQ, HEAD),
            P(SEQ, HEAD),
            P(None, HEAD),
            P(None, HEAD),
            P(),
        ),
        check_vma=False,
    )


FINE_SIZES = None
```

```python
import functools
import math

import jax
import jax.numpy as jnp
import numpy as np
from jax import lax
from jax.experimental import pallas as pl
from jax.experimental.pallas import tpu as pltpu
from jax.sharding import Mesh
from jax.sharding import PartitionSpec as P


HEAD_DIM = 128
TILE_H = 8
TILE_W = 8
SECTIONS = ((0, 16), (16, 56), (72, 56))
THETA = 256.0
SCALE = HEAD_DIM ** -0.5
LOG2E = math.log2(math.e)
C1 = SCALE * LOG2E
SEQ = ("z", "y", "core")
COL = ("y", "core")
HEAD = ("yhi", "x")
F32 = jnp.float32
BF16 = jnp.bfloat16
NEG = -1e30
VMEM_LIMIT = 66_000_000


def dot_nn(a, b):
    return lax.dot_general(a, b, (((1,), (0,)), ((), ())), preferred_element_type=F32)


def dot_nt(a, b):
    return lax.dot_general(a, b, (((1,), (1,)), ((), ())), preferred_element_type=F32)


def dot_tn(a, b):
    return lax.dot_general(a, b, (((0,), (0,)), ((), ())), preferred_element_type=F32)


def params(*semantics):
    return pltpu.CompilerParams(
        dimension_semantics=semantics or None, vmem_limit_bytes=VMEM_LIMIT
    )


def lane_freqs():
    freqs = np.zeros((8, HEAD_DIM), np.float32)
    for offset, length in SECTIONS:
        half = length // 2
        f = np.float32(THETA) ** (
            np.float32(-2.0) * np.arange(half, dtype=np.float32) / np.float32(length)
        )
        freqs[:, offset : offset + half] = f
        freqs[:, offset + half : offset + length] = f
    return freqs


def partner(x, lane):
    near = jnp.where(lane < 8, pltpu.roll(x, HEAD_DIM - 8, 1), pltpu.roll(x, 8, 1))
    first = ((lane >= 16) & (lane < 44)) | ((lane >= 72) & (lane < 100))
    far = jnp.where(first, pltpu.roll(x, HEAD_DIM - 28, 1), pltpu.roll(x, 28, 1))
    return jnp.where(lane < 16, near, far)


def whole(shape):
    return pl.BlockSpec(shape, lambda *_: (0,) * len(shape))


def smem():
    return pl.BlockSpec(memory_space=pltpu.SMEM)


def rot_kernel(info, freq, q, k, v, q_out, kv_out, cos_out, sin_out):
    tile = q.shape[0]

    @pl.when(pl.program_id(0) == 0)
    def _():
        frames = tile // (TILE_H * TILE_W)
        step = lax.broadcasted_iota(jnp.int32, (8, HEAD_DIM), 0)
        lane = lax.broadcasted_iota(jnp.int32, (8, HEAD_DIM), 1)
        first = (
            (lane < 8) | ((lane >= 16) & (lane < 44)) | ((lane >= 72) & (lane < 100))
        )
        f = freq[...]

        def table(base):
            angle = (base + step).astype(F32) * f
            s = jnp.sin(angle)
            return jnp.cos(angle), jnp.where(first, -s, s)

        cf, sf = table(info[4] * frames)
        cr, sr = table(info[5] * TILE_H)
        cc, sc = table(info[6] * TILE_W)
        for r in range(TILE_H):
            crr = jnp.where(lane < 72, cr[r : r + 1, :], cc)
            srr = jnp.where(lane < 72, sr[r : r + 1, :], sc)
            for t in range(frames):
                at = (t * TILE_H + r) * TILE_W
                cos_out[at : at + TILE_W, :] = jnp.where(lane < 16, cf[t : t + 1, :], crr)
                sin_out[at : at + TILE_W, :] = jnp.where(lane < 16, sf[t : t + 1, :], srr)

    lane = lax.broadcasted_iota(jnp.int32, (tile, HEAD_DIM), 1)
    cos, sin = cos_out[...], sin_out[...]
    for source, target in ((q, q_out), (k, kv_out.at[0])):
        x = source[...].astype(F32)
        target[...] = (x * cos + partner(x, lane) * sin).astype(BF16)
    kv_out[1] = v[...]


def rotate_call(info, q_in, k_in, v_in):
    tile, width = q_in.shape
    heads = width // HEAD_DIM
    half = pl.BlockSpec((tile, HEAD_DIM), lambda h: (0, h))
    table = whole((tile, HEAD_DIM))
    return pl.pallas_call(
        rot_kernel,
        grid=(heads,),
        in_specs=[smem(), whole((8, HEAD_DIM)), half, half, half],
        out_specs=[half, pl.BlockSpec((2, tile, HEAD_DIM), lambda h: (0, 0, h)), table, table],
        out_shape=[
            jax.ShapeDtypeStruct((tile, width), BF16),
            jax.ShapeDtypeStruct((2, tile, width), BF16),
            jax.ShapeDtypeStruct((tile, HEAD_DIM), F32),
            jax.ShapeDtypeStruct((tile, HEAD_DIM), F32),
        ],
        compiler_params=params("arbitrary"),
        name="rot",
    )(info, jnp.asarray(lane_freqs()), q_in, k_in, v_in)


def open_block(info, h, a, b):
    ok = (info[8 + 2 * h] >= abs(a)) & (info[9 + 2 * h] >= abs(b))
    if a:
        row = info[0] + a
        ok = ok & (row >= 0) & (row < info[2])
    if b:
        col = info[1] + b
        ok = ok & (col >= 0) & (col < info[3])
    return ok


def fwd_block(keys, values, extra, q, m, l, acc):
    s = dot_nt(keys, q[...]) * C1
    if extra is not None:
        s = s + extra
    m_old = m[0:1, :]
    m_new = jnp.maximum(m_old, jnp.max(s, axis=0, keepdims=True))
    p = jnp.exp2(s - m_new)
    alpha = jnp.exp2(m_old - m_new)
    m[0:1, :] = m_new
    l[0:1, :] = l[0:1, :] * alpha + jnp.sum(p, axis=0, keepdims=True)
    acc[...] = acc[...] * alpha + dot_tn(values, p.astype(BF16))


def fwd_near_kernel(info, q, own, up, down, tk, tv, bias, acc, m, l):
    h = pl.program_id(0)
    m[...] = jnp.full(m.shape, NEG, F32)
    l[...] = jnp.zeros(l.shape, F32)
    acc[...] = jnp.zeros(acc.shape, F32)
    fwd_block(own[0], own[1], None, q, m, l, acc)
    fwd_block(tk[...], tv[...], bias[...], q, m, l, acc)
    for a, ref in ((-1, up), (1, down)):

        @pl.when(open_block(info, h, a, 0))
        def _(ref=ref):
            fwd_block(ref[0], ref[1], None, q, m, l, acc)


def fwd_side_kernel(info, q, left, right, acc_in, m_in, l_in, ot_out, lse_out, acc, m, l):
    h = pl.program_id(0)
    acc[...] = acc_in[...]
    m[...] = m_in[...]
    l[...] = l_in[...]
    for b, ref in ((-1, left), (1, right)):
        for a in (-1, 0, 1):

            @pl.when(open_block(info, h, a, b))
            def _(ref=ref, a=a):
                fwd_block(ref[a + 1, 0], ref[a + 1, 1], None, q, m, l, acc)

    ot_out[...] = (acc[...] * (1.0 / l[0:1, :])).astype(BF16)
    lse_out[...] = jnp.broadcast_to(m[0:1, :] + jnp.log2(l[0:1, :]), lse_out.shape)


def kv_spec(tile):
    return pl.BlockSpec((2, tile, HEAD_DIM), lambda h: (0, 0, h))


def stack_spec(tile):
    return pl.BlockSpec((3, 2, tile, HEAD_DIM), lambda h: (0, 0, 0, h))


def half_spec(rows):
    return pl.BlockSpec((rows, HEAD_DIM), lambda h: (0, h))


def row_spec(rows, tile):
    return pl.BlockSpec((rows, tile), lambda h: (h, 0))


def fwd_near_call(info, q, own, up, down, text_keys, text_values, bias):
    tile, width = q.shape
    heads = width // HEAD_DIM
    txt = text_keys.shape[0]
    keys = 3 * tile + txt
    stats = jax.ShapeDtypeStruct((8 * heads, tile), F32)
    return pl.pallas_call(
        fwd_near_kernel,
        grid=(heads,),
        in_specs=[smem(), half_spec(tile)]
        + [kv_spec(tile)] * 3
        + [half_spec(txt), half_spec(txt), whole((txt, 1))],
        out_specs=[row_spec(HEAD_DIM, tile), row_spec(8, tile), row_spec(8, tile)],
        out_shape=[jax.ShapeDtypeStruct((width, tile), F32), stats, stats],
        compiler_params=params("arbitrary"),
        cost_estimate=pl.CostEstimate(
            flops=4 * tile * keys * width, bytes_accessed=4 * keys * width, transcendentals=0
        ),
        name="fwd_near",
    )(info, q, own, up, down, text_keys, text_values, bias)


def fwd_side_call(info, q, left, right, acc, m, l):
    tile, width = q.shape
    heads = width // HEAD_DIM
    keys = 6 * tile
    return pl.pallas_call(
        fwd_side_kernel,
        grid=(heads,),
        in_specs=[
            smem(),
            half_spec(tile),
            stack_spec(tile),
            stack_spec(tile),
            row_spec(HEAD_DIM, tile),
            row_spec(8, tile),
            row_spec(8, tile),
        ],
        out_specs=[row_spec(HEAD_DIM, tile), row_spec(8, tile)],
        out_shape=[
            jax.ShapeDtypeStruct((width, tile), BF16),
            jax.ShapeDtypeStruct((8 * heads, tile), F32),
        ],
        scratch_shapes=[
            pltpu.VMEM((HEAD_DIM, tile), F32),
            pltpu.VMEM((8, tile), F32),
            pltpu.VMEM((8, tile), F32),
        ],
        compiler_params=params("arbitrary"),
        cost_estimate=pl.CostEstimate(
            flops=4 * tile * keys * width, bytes_accessed=4 * keys * width, transcendentals=0
        ),
        name="fwd_side",
    )(info, q, left, right, acc, m, l)


def stack_kernel(up, own, down, out):
    out[0] = up[...]
    out[1] = own[...]
    out[2] = down[...]


def stack_call(up, own, down):
    tile, width = own.shape[1:]
    return pl.pallas_call(
        stack_kernel,
        grid=(width // HEAD_DIM,),
        in_specs=[kv_spec(tile)] * 3,
        out_specs=stack_spec(tile),
        out_shape=jax.ShapeDtypeStruct((3, 2, tile, width), BF16),
        compiler_params=params("arbitrary"),
        name="stack",
    )(up, own, down)


def proj_kernel(steps, last, info, w, gate, ot, *refs):
    pieces, rest = refs[: len(steps)], refs[len(steps) :]
    if last:
        acc_in, gate_in, dot_out, delta_out, gate_out = rest
    else:
        acc_out, gate_out = rest
    heads_x, heads_y = info[16], info[17]
    acc = acc_in[...] if last else None
    if last:
        gate_out[...] = gate_in[...]
    else:
        gate_out[...] = jnp.zeros(gate_out.shape, F32)
    tile = ot.shape[1]
    for piece, (flip, dx) in zip(pieces, steps):
        y = info[18] if not flip else heads_y - 1 - info[18]
        x = lax.rem(info[19] + dx + heads_x, heads_x)
        block = y * heads_x + x
        cols = piece.shape[1]
        at = pl.multiple_of(block * cols, 128)
        g = piece[...].astype(F32)
        scaled = (g * gate[:, pl.ds(at, cols)]).astype(BF16)
        wp = w[:, pl.ds(at, cols)]
        part = dot_nt(wp, scaled)
        acc = part if acc is None else acc + part
        terms = dot_nn(ot[...], piece[...]) * wp.astype(F32)
        row = jnp.sum(terms, axis=0, keepdims=True)
        for i in range(cols // 128):
            gate_out[pl.ds(block * (cols // 128) + i, 1), :] = row[:, i * 128 : (i + 1) * 128]
    if not last:
        acc_out[...] = acc
    else:
        rounded = acc.astype(BF16)
        dot_out[...] = rounded
        prod = rounded.astype(F32) * ot[...].astype(F32)
        for h in range(ot.shape[0] // HEAD_DIM):
            d = jnp.sum(prod[h * HEAD_DIM : (h + 1) * HEAD_DIM, :], axis=0, keepdims=True)
            delta_out[8 * h : 8 * h + 8, :] = jnp.broadcast_to(d, (8, tile))


def proj_call(steps, info, w, gate, ot, pieces, carried=None):
    width, tile = ot.shape
    heads = width // HEAD_DIM
    cols = pieces[0].shape[1]
    rows = w.shape[1] // 128
    last = carried is not None
    acc = jax.ShapeDtypeStruct((width, tile), F32)
    gates = jax.ShapeDtypeStruct((rows, 128), F32)
    if last:
        out_shape = [
            jax.ShapeDtypeStruct((width, tile), BF16),
            jax.ShapeDtypeStruct((8 * heads, tile), F32),
            gates,
        ]
    else:
        out_shape = [acc, gates]
    operands = (info, w, gate, ot, *pieces) + (tuple(carried) if last else ())
    return pl.pallas_call(
        functools.partial(proj_kernel, steps, last),
        in_specs=[smem()] + [pl.BlockSpec(memory_space=pltpu.VMEM)] * (len(operands) - 1),
        out_specs=[pl.BlockSpec(memory_space=pltpu.VMEM)] * len(out_shape),
        out_shape=out_shape,
        compiler_params=params(),
        cost_estimate=pl.CostEstimate(
            flops=4 * tile * width * cols * len(pieces),
            bytes_accessed=2 * tile * cols * len(pieces) + 2 * w.size,
            transcendentals=0,
        ),
        name="proj",
    )(*operands)


def bwd_math(keys, values, q, dot, lse, delta, dq, extra):
    s = dot_nt(keys, q[...]) * C1
    if extra is not None:
        s = s + extra
    p = jnp.exp2(s - lse[0:1, :])
    dp = dot_nn(values, dot[...])
    ds = (p * (dp - delta[0:1, :])).astype(BF16)
    dv = dot_nt(p.astype(BF16), dot[...])
    dk = dot_nn(ds, q[...]) * SCALE
    dq[...] += dot_tn(keys, ds)
    return dk, dv


def bwd_block(info, h, a, b, block, out, q, dot, lse, delta, dq):
    def run():
        dk, dv = bwd_math(block[0], block[1], q, dot, lse, delta, dq, None)
        out[0] = dk.astype(out.dtype)
        out[1] = dv.astype(out.dtype)

    if (a, b) == (0, 0):
        run()
    else:
        ok = open_block(info, h, a, b)
        pl.when(ok)(run)

        @pl.when(jnp.logical_not(ok))
        def _():
            out[...] = jnp.zeros(out.shape, out.dtype)


def bwd_side_kernel(
    info, q, dot, lse, delta, tk, tv, bias, left, right, left_out, right_out, text_out, dq_out
):
    h = pl.program_id(0)
    dq_out[...] = jnp.zeros(dq_out.shape, F32)
    dk, dv = bwd_math(tk[...], tv[...], q, dot, lse, delta, dq_out, bias[...])
    text_out[0] = dk.astype(BF16)
    text_out[1] = dv.astype(BF16)
    for b, ref, out in ((-1, left, left_out), (1, right, right_out)):
        for a in (-1, 0, 1):
            bwd_block(
                info, h, a, b, ref.at[a + 1], out.at[a + 1], q, dot, lse, delta, dq_out
            )


def bwd_near_kernel(
    info, q, dot, lse, delta, dq_in, cos, sin, up, own, down, up_out, own_out, down_out, gq_out, dq
):
    h = pl.program_id(0)
    dq[...] = dq_in[...]
    for a, ref, out in ((-1, up, up_out), (1, down, down_out), (0, own, own_out)):
        bwd_block(info, h, a, 0, ref, out, q, dot, lse, delta, dq)
    x = jnp.transpose(dq[...]) * SCALE
    lane = lax.broadcasted_iota(jnp.int32, x.shape, 1)
    gq_out[...] = (x * cos[...] - partner(x, lane) * sin[...]).astype(BF16)


def bwd_specs(tile):
    return [
        smem(),
        pl.BlockSpec((tile, HEAD_DIM), lambda h: (0, h)),
        pl.BlockSpec((HEAD_DIM, tile), lambda h: (h, 0)),
        pl.BlockSpec((8, tile), lambda h: (h, 0)),
        pl.BlockSpec((8, tile), lambda h: (h, 0)),
    ]


def bwd_cost(tile, keys, width):
    return pl.CostEstimate(
        flops=10 * tile * keys * width, bytes_accessed=8 * keys * width, transcendentals=0
    )


def bwd_side_call(common, text_keys, text_values, bias, left, right):
    info, q, dot, lse, delta = common
    tile, width = q.shape
    txt = text_keys.shape[0]
    stack = jax.ShapeDtypeStruct((3, 2, tile, width), BF16)
    return pl.pallas_call(
        bwd_side_kernel,
        grid=(width // HEAD_DIM,),
        in_specs=bwd_specs(tile)
        + [half_spec(txt), half_spec(txt), whole((txt, 1))]
        + [stack_spec(tile)] * 2,
        out_specs=[stack_spec(tile)] * 2 + [kv_spec(txt), row_spec(HEAD_DIM, tile)],
        out_shape=[
            stack,
            stack,
            jax.ShapeDtypeStruct((2, txt, width), BF16),
            jax.ShapeDtypeStruct((width, tile), F32),
        ],
        compiler_params=params("arbitrary"),
        cost_estimate=bwd_cost(tile, 6 * tile + txt, width),
        name="bwd_side",
    )(info, q, dot, lse, delta, text_keys, text_values, bias, left, right)


def bwd_near_call(common, dq, cos, sin, up, own, down):
    info, q, dot, lse, delta = common
    tile, width = q.shape
    table = whole((tile, HEAD_DIM))
    part = jax.ShapeDtypeStruct((2, tile, width), F32)
    return pl.pallas_call(
        bwd_near_kernel,
        grid=(width // HEAD_DIM,),
        in_specs=bwd_specs(tile)
        + [row_spec(HEAD_DIM, tile), table, table]
        + [kv_spec(tile)] * 3,
        out_specs=[kv_spec(tile)] * 3 + [half_spec(tile)],
        out_shape=[part, part, part, jax.ShapeDtypeStruct((tile, width), BF16)],
        scratch_shapes=[pltpu.VMEM((HEAD_DIM, tile), F32)],
        compiler_params=params("arbitrary"),
        cost_estimate=bwd_cost(tile, 3 * tile, width),
        name="bwd_near",
    )(info, q, dot, lse, delta, dq, cos, sin, up, own, down)


def pair_sum_kernel(up, down, left, right, up_out, down_out):
    for i, part, out in ((0, up, up_out), (2, down, down_out)):
        out[...] = (part[...] + left[i].astype(F32) + right[i].astype(F32)).astype(BF16)


def pair_sum_call(up, down, left, right):
    tile, width = up.shape[1:]
    shape = jax.ShapeDtypeStruct((2, tile, width), BF16)
    return pl.pallas_call(
        pair_sum_kernel,
        grid=(width // HEAD_DIM,),
        in_specs=[kv_spec(tile)] * 2 + [stack_spec(tile)] * 2,
        out_specs=[kv_spec(tile)] * 2,
        out_shape=[shape] * 2,
        compiler_params=params("arbitrary"),
        name="pair_sum",
    )(up, down, left, right)


def finish_kernel(own, left, right, up, down, cos, sin, gk_out, gv_out):
    total = own[...]
    for other in (left[0], right[0], up[...], down[...]):
        total = total + other.astype(F32)
    x = total[0]
    lane = lax.broadcasted_iota(jnp.int32, x.shape, 1)
    gk_out[...] = (x * cos[...] - partner(x, lane) * sin[...]).astype(BF16)
    gv_out[...] = total[1].astype(BF16)


def finish_call(own, left, right, up, down, cos, sin):
    tile, width = own.shape[1:]
    table = whole((tile, HEAD_DIM))
    middle = pl.BlockSpec((1, 2, tile, HEAD_DIM), lambda h: (1, 0, 0, h))
    shape = jax.ShapeDtypeStruct((tile, width), BF16)
    return pl.pallas_call(
        finish_kernel,
        grid=(width // HEAD_DIM,),
        in_specs=[kv_spec(tile), middle, middle, kv_spec(tile), kv_spec(tile), table, table],
        out_specs=[half_spec(tile)] * 2,
        out_shape=[shape, shape],
        compiler_params=params("arbitrary"),
        name="finish",
    )(own, left, right, up, down, cos, sin)


def chunk_sum_kernel(got, gate, out):
    groups, rows, width = got.shape
    text = jnp.sum(got[...].astype(F32), axis=0).astype(BF16)
    out[:, :, :width] = jnp.broadcast_to(text[None], (groups, rows, width))
    for i in range(gate.shape[0] // rows):
        part = gate[i * rows : (i + 1) * rows, :].astype(BF16)
        at = width + 128 * i
        out[:, :, at : at + 128] = jnp.broadcast_to(part[None], (groups, rows, 128))


def chunk_sum_call(got, gate):
    groups, rows, width = got.shape
    lanes = width + 128 * (gate.shape[0] // rows)
    return pl.pallas_call(
        chunk_sum_kernel,
        in_specs=[pl.BlockSpec(memory_space=pltpu.VMEM)] * 2,
        out_specs=pl.BlockSpec(memory_space=pltpu.VMEM),
        out_shape=jax.ShapeDtypeStruct((groups, rows, lanes), BF16),
        compiler_params=params(),
        name="chunk_sum",
    )(got, gate)


def unpack_kernel(got, keys_out, values_out, gate_out):
    groups, rows, _ = got.shape
    width = keys_out.shape[1]
    half = groups // 2
    keys_out[...] = got[:half, :, :width].reshape(half * rows, width)
    values_out[...] = got[half:, :, :width].reshape(half * rows, width)
    for i in range(gate_out.shape[0] // rows):
        at = width + 128 * i
        gate_out[i * rows : (i + 1) * rows, :] = jnp.sum(
            got[:, :, at : at + 128].astype(F32), axis=0
        )


def unpack_call(got, width, gate_rows):
    groups, rows, _ = got.shape
    text = jax.ShapeDtypeStruct((groups // 2 * rows, width), BF16)
    return pl.pallas_call(
        unpack_kernel,
        in_specs=[pl.BlockSpec(memory_space=pltpu.VMEM)],
        out_specs=[pl.BlockSpec(memory_space=pltpu.VMEM)] * 3,
        out_shape=[text, text, jax.ShapeDtypeStruct((gate_rows, 128), F32)],
        compiler_params=params(),
        name="unpack",
    )(got)


def shift(array, axis, by, wrap=False):
    length = lax.axis_size(axis)
    pairs = [(i, (i + by) % length) for i in range(length) if wrap or 0 <= i + by < length]
    return lax.ppermute(array, axis, pairs)


def swap(array, axis, bit):
    length = lax.axis_size(axis)
    return lax.ppermute(array, axis, [(i, i ^ bit) for i in range(length)])


def in_hbm(*arrays):
    return [pltpu.with_memory_space_constraint(a, pltpu.HBM) for a in arrays]


def on_device(
    query_in,
    key_in,
    value_in,
    text_keys,
    text_values,
    text_mask,
    window_reach,
    tile_map,
    out_weight,
    gate_scale,
    grad_out,
):
    _, width = query_in.shape
    seq_count = lax.axis_size(SEQ)
    row, col = lax.axis_index("z"), lax.axis_index(COL)
    coords = lax.dynamic_slice(tile_map, (lax.axis_index(SEQ), 0), (1, 3))[0]
    counts = jnp.array(
        [lax.axis_size("z"), lax.axis_size(COL)], jnp.int32
    )
    info = jnp.concatenate(
        [
            jnp.stack([row, col]).astype(jnp.int32),
            counts,
            coords,
            jnp.zeros((1,), jnp.int32),
            window_reach.reshape(-1),
            jnp.zeros((8 - window_reach.size,), jnp.int32),
            jnp.array([lax.axis_size("x"), lax.axis_size("yhi")], jnp.int32),
            jnp.stack([lax.axis_index("yhi"), lax.axis_index("x")]).astype(jnp.int32),
        ]
    )
    bias = jnp.where(text_mask == 1, 0.0, NEG).astype(F32)[:, None]

    query_in, key_in, value_in = in_hbm(query_in, key_in, value_in)
    text_keys, text_values = in_hbm(text_keys, text_values)

    g_y = swap(grad_out, "yhi", 1)
    g_r = shift(grad_out, "x", 1, True)
    g_l = shift(grad_out, "x", -1, True)

    q, kv, cos, sin = rotate_call(info, query_in, key_in, value_in)

    kv_up, kv_down = shift(kv, "z", 1), shift(kv, "z", -1)
    g_far = shift(g_l, "x", -1, True)
    gy_r = shift(g_y, "x", 1, True)
    gy_l = shift(g_y, "x", -1, True)
    stack = stack_call(kv_up, kv, kv_down)
    kv_left, kv_right = shift(stack, COL, 1), shift(stack, COL, -1)
    gy_far = shift(gy_r, "x", 1, True)

    partial = fwd_near_call(info, q, kv, kv_up, kv_down, text_keys, text_values, bias)
    ot, lse = fwd_side_call(info, q, kv_left, kv_right, *partial)

    gate = gate_scale.reshape(1, -1)
    steps = ((False, 0), (False, -1), (False, 1), (False, 2))
    carried = proj_call(steps, info, out_weight, gate, ot, [grad_out, g_r, g_l, g_far])
    steps = ((True, 0), (True, -1), (True, 1), (True, 2))
    dot, delta, gate_terms = proj_call(
        steps, info, out_weight, gate, ot, [g_y, gy_r, gy_l, gy_far], carried
    )

    common = (info, q, dot, lse, delta)
    left, right, text_part, dq = bwd_side_call(
        common, text_keys, text_values, bias, kv_left, kv_right
    )
    back_left = shift(left, COL, -1)
    back_right = shift(right, COL, 1)
    got = lax.all_to_all(
        text_part.reshape(seq_count, -1, width), SEQ, 0, 0, tiled=True
    )
    up, own, down, grad_query = bwd_near_call(common, dq, cos, sin, kv_up, kv, kv_down)
    for axis in ("x", "yhi"):
        bit = 1
        while bit < lax.axis_size(axis):
            gate_terms = gate_terms + swap(gate_terms, axis, bit)
            bit *= 2

    up, down = pair_sum_call(up, down, back_left, back_right)
    up = shift(up, "z", -1)
    down = shift(down, "z", 1)

    chunk = chunk_sum_call(got, gate_terms)
    summed = lax.all_to_all(chunk, SEQ, 0, 0, tiled=True)
    grad_text_keys, grad_text_values, grad_gate = unpack_call(
        summed, width, out_weight.shape[1] // 128
    )
    grad_key, grad_value = finish_call(own, back_left, back_right, up, down, cos, sin)
    return (
        grad_query,
        grad_key,
        grad_value,
        grad_text_keys,
        grad_text_values,
        grad_gate.reshape(-1),
    )


def solution(mesh):
    fine = Mesh(mesh.devices.reshape(SIZES), (*SEQ, *HEAD))
    head = P(SEQ, HEAD)
    placed = (
        head,
        head,
        head,
        P(None, HEAD),
        P(None, HEAD),
        P(),
        P(HEAD, None),
        P(),
        P(HEAD, None),
        P(),
        head,
    )

    return jax.shard_map(
        on_device,
        mesh=fine,
        in_specs=placed,
        out_specs=(head, head, head, P(None, HEAD), P(None, HEAD), P()),
        check_vma=False,
    )


SIZES = (8, 4, 2, 2, 4)
```

```python
import functools
import math

import jax
import jax.numpy as jnp
import numpy as np
from jax import lax
from jax.experimental import pallas as pl
from jax.experimental.pallas import tpu as pltpu
from jax.sharding import Mesh
from jax.sharding import PartitionSpec as P


HEAD_DIM = 128
TILE_H = 8
TILE_W = 8
SECTIONS = ((0, 16), (16, 56), (72, 56))
THETA = 256.0
SCALE = HEAD_DIM ** -0.5
LOG2E = math.log2(math.e)
C1 = SCALE * LOG2E
SEQ = ("z", "y", "core")
COL = ("y", "core")
HEAD = ("yhi", "x")
F32 = jnp.float32
BF16 = jnp.bfloat16
NEG = -1e30
VMEM_LIMIT = 66_000_000
SMALL = 16_000_000


def dot_nn(a, b):
    return lax.dot_general(a, b, (((1,), (0,)), ((), ())), preferred_element_type=F32)


def dot_nt(a, b):
    return lax.dot_general(a, b, (((1,), (1,)), ((), ())), preferred_element_type=F32)


def dot_tn(a, b):
    return lax.dot_general(a, b, (((0,), (0,)), ((), ())), preferred_element_type=F32)


def params(*semantics, limit=VMEM_LIMIT):
    return pltpu.CompilerParams(
        dimension_semantics=semantics or None, vmem_limit_bytes=limit
    )


def lane_freqs():
    freqs = np.zeros((8, HEAD_DIM), np.float32)
    for offset, length in SECTIONS:
        half = length // 2
        f = np.float32(THETA) ** (
            np.float32(-2.0) * np.arange(half, dtype=np.float32) / np.float32(length)
        )
        freqs[:, offset : offset + half] = f
        freqs[:, offset + half : offset + length] = f
    return freqs


def partner(x, lane):
    near = jnp.where(lane < 8, pltpu.roll(x, HEAD_DIM - 8, 1), pltpu.roll(x, 8, 1))
    first = ((lane >= 16) & (lane < 44)) | ((lane >= 72) & (lane < 100))
    far = jnp.where(first, pltpu.roll(x, HEAD_DIM - 28, 1), pltpu.roll(x, 28, 1))
    return jnp.where(lane < 16, near, far)


def whole(shape):
    return pl.BlockSpec(shape, lambda *_: (0,) * len(shape))


def smem():
    return pl.BlockSpec(memory_space=pltpu.SMEM)


def rot_kernel(sizes, reach, tiles, freq, q, k, v, q_out, kv_out, cos_out, sin_out, info):
    tile = q.shape[0]

    @pl.when(pl.program_id(0) == 0)
    def _():
        rows, ys, cores, _, _ = sizes
        row = lax.axis_index("z")
        col = lax.axis_index("y") * cores + lax.axis_index("core")
        info[0] = row
        info[1] = col
        info[2] = rows
        info[3] = ys * cores
        info[4] = lax.axis_index("yhi")
        for h in range(reach.shape[0]):
            info[8 + 2 * h] = reach[h, 0]
            info[9 + 2 * h] = reach[h, 1]
        own = row * (ys * cores) + col
        frames = tile // (TILE_H * TILE_W)
        step = lax.broadcasted_iota(jnp.int32, (8, HEAD_DIM), 0)
        lane = lax.broadcasted_iota(jnp.int32, (8, HEAD_DIM), 1)
        first = (
            (lane < 8) | ((lane >= 16) & (lane < 44)) | ((lane >= 72) & (lane < 100))
        )
        f = freq[...]

        def table(base):
            angle = (base + step).astype(F32) * f
            s = jnp.sin(angle)
            return jnp.cos(angle), jnp.where(first, -s, s)

        cf, sf = table(tiles[0, own] * frames)
        cr, sr = table(tiles[1, own] * TILE_H)
        cc, sc = table(tiles[2, own] * TILE_W)
        for r in range(TILE_H):
            crr = jnp.where(lane < 72, cr[r : r + 1, :], cc)
            srr = jnp.where(lane < 72, sr[r : r + 1, :], sc)
            for t in range(frames):
                at = (t * TILE_H + r) * TILE_W
                cos_out[at : at + TILE_W, :] = jnp.where(lane < 16, cf[t : t + 1, :], crr)
                sin_out[at : at + TILE_W, :] = jnp.where(lane < 16, sf[t : t + 1, :], srr)

    lane = lax.broadcasted_iota(jnp.int32, (tile, HEAD_DIM), 1)
    cos, sin = cos_out[...], sin_out[...]
    for source, target in ((q, q_out), (k, kv_out.at[0])):
        x = source[...].astype(F32)
        target[...] = (x * cos + partner(x, lane) * sin).astype(BF16)
    kv_out[1] = v[...]


def rotate_call(sizes, reach, tile_map, q_in, k_in, v_in):
    tile, width = q_in.shape
    heads = width // HEAD_DIM
    half = pl.BlockSpec((tile, HEAD_DIM), lambda h: (0, h))
    table = whole((tile, HEAD_DIM))
    return pl.pallas_call(
        functools.partial(rot_kernel, sizes),
        grid=(heads,),
        in_specs=[smem(), smem(), whole((8, HEAD_DIM)), half, half, half],
        out_specs=[half, kv_spec(tile), table, table, smem()],
        out_shape=[
            jax.ShapeDtypeStruct((tile, width), BF16),
            jax.ShapeDtypeStruct((2, tile, width), BF16),
            jax.ShapeDtypeStruct((tile, HEAD_DIM), F32),
            jax.ShapeDtypeStruct((tile, HEAD_DIM), F32),
            jax.ShapeDtypeStruct((24,), jnp.int32),
        ],
        compiler_params=params("arbitrary"),
        name="rot",
    )(reach, tile_map.T, jnp.asarray(lane_freqs()), q_in, k_in, v_in)


def open_block(info, h, a, b):
    ok = (info[8 + 2 * h] >= abs(a)) & (info[9 + 2 * h] >= abs(b))
    if a:
        row = info[0] + a
        ok = ok & (row >= 0) & (row < info[2])
    if b:
        col = info[1] + b
        ok = ok & (col >= 0) & (col < info[3])
    return ok


def mask_column(mask):
    closed = jnp.where(mask[...] == 1, 0.0, NEG).astype(F32)
    return jnp.transpose(jnp.broadcast_to(closed, (8, closed.shape[1])))[:, 0:1]


def fwd_block(keys, values, extra, q, m, l, acc):
    s = dot_nt(keys, q[...]) * C1
    if extra is not None:
        s = s + extra
    m_old = m[0:1, :]
    m_new = jnp.maximum(m_old, jnp.max(s, axis=0, keepdims=True))
    p = jnp.exp2(s - m_new)
    alpha = jnp.exp2(m_old - m_new)
    m[0:1, :] = m_new
    l[0:1, :] = l[0:1, :] * alpha + jnp.sum(p, axis=0, keepdims=True)
    acc[...] = acc[...] * alpha + dot_tn(values, p.astype(BF16))


def fwd_near_kernel(info, q, own, up, down, tk, tv, mask, acc, m, l):
    h = pl.program_id(0)
    m[...] = jnp.full(m.shape, NEG, F32)
    l[...] = jnp.zeros(l.shape, F32)
    acc[...] = jnp.zeros(acc.shape, F32)
    fwd_block(own[0], own[1], None, q, m, l, acc)
    fwd_block(tk[...], tv[...], mask_column(mask), q, m, l, acc)
    for a, ref in ((-1, up), (1, down)):

        @pl.when(open_block(info, h, a, 0))
        def _(ref=ref):
            fwd_block(ref[0], ref[1], None, q, m, l, acc)


def fwd_side_kernel(info, q, left, right, acc_in, m_in, l_in, ot_out, lse_out, acc, m, l):
    h = pl.program_id(0)
    acc[...] = acc_in[...]
    m[...] = m_in[...]
    l[...] = l_in[...]
    for b, ref in ((-1, left), (1, right)):
        for a in (-1, 0, 1):

            @pl.when(open_block(info, h, a, b))
            def _(ref=ref, a=a):
                fwd_block(ref[a + 1, 0], ref[a + 1, 1], None, q, m, l, acc)

    ot_out[...] = (acc[...] * (1.0 / l[0:1, :])).astype(BF16)
    lse_out[...] = jnp.broadcast_to(m[0:1, :] + jnp.log2(l[0:1, :]), lse_out.shape)


def kv_spec(tile):
    return pl.BlockSpec((2, tile, HEAD_DIM), lambda h: (0, 0, h))


def stack_spec(tile):
    return pl.BlockSpec((3, 2, tile, HEAD_DIM), lambda h: (0, 0, 0, h))


def half_spec(rows):
    return pl.BlockSpec((rows, HEAD_DIM), lambda h: (0, h))


def row_spec(rows, tile):
    return pl.BlockSpec((rows, tile), lambda h: (h, 0))


def fwd_near_call(info, q, own, up, down, text_keys, text_values, mask):
    tile, width = q.shape
    heads = width // HEAD_DIM
    txt = text_keys.shape[0]
    keys = 3 * tile + txt
    stats = jax.ShapeDtypeStruct((8 * heads, tile), F32)
    return pl.pallas_call(
        fwd_near_kernel,
        grid=(heads,),
        in_specs=[smem(), half_spec(tile)]
        + [kv_spec(tile)] * 3
        + [half_spec(txt), half_spec(txt), whole((1, txt))],
        out_specs=[row_spec(HEAD_DIM, tile), row_spec(8, tile), row_spec(8, tile)],
        out_shape=[jax.ShapeDtypeStruct((width, tile), F32), stats, stats],
        compiler_params=params("arbitrary"),
        cost_estimate=pl.CostEstimate(
            flops=4 * tile * keys * width, bytes_accessed=4 * keys * width, transcendentals=0
        ),
        name="fwd_near",
    )(info, q, own, up, down, text_keys, text_values, mask)


def fwd_side_call(info, q, left, right, acc, m, l):
    tile, width = q.shape
    heads = width // HEAD_DIM
    keys = 6 * tile
    return pl.pallas_call(
        fwd_side_kernel,
        grid=(heads,),
        in_specs=[
            smem(),
            half_spec(tile),
            stack_spec(tile),
            stack_spec(tile),
            row_spec(HEAD_DIM, tile),
            row_spec(8, tile),
            row_spec(8, tile),
        ],
        out_specs=[row_spec(HEAD_DIM, tile), row_spec(8, tile)],
        out_shape=[
            jax.ShapeDtypeStruct((width, tile), BF16),
            jax.ShapeDtypeStruct((8 * heads, tile), F32),
        ],
        scratch_shapes=[
            pltpu.VMEM((HEAD_DIM, tile), F32),
            pltpu.VMEM((8, tile), F32),
            pltpu.VMEM((8, tile), F32),
        ],
        compiler_params=params("arbitrary"),
        cost_estimate=pl.CostEstimate(
            flops=4 * tile * keys * width, bytes_accessed=4 * keys * width, transcendentals=0
        ),
        name="fwd_side",
    )(info, q, left, right, acc, m, l)


def stack_kernel(up, own, down, out):
    out[0] = up[...]
    out[1] = own[...]
    out[2] = down[...]


def stack_call(up, own, down):
    tile, width = own.shape[1:]
    return pl.pallas_call(
        stack_kernel,
        grid=(width // HEAD_DIM,),
        in_specs=[kv_spec(tile)] * 3,
        out_specs=stack_spec(tile),
        out_shape=jax.ShapeDtypeStruct((3, 2, tile, width), BF16),
        compiler_params=params("arbitrary", limit=SMALL),
        name="stack",
    )(up, own, down)


def piece_block(info, flip, ys, xs, x):
    y = ys - 1 - info[4] if flip else info[4]
    return y * xs + x


def proj_kernel(flip, ys, xs, info, w, gate, ot, piece, *refs):
    if flip:
        acc_in, gate_in, dot_out, delta_out, gate_out, acc, gates = refs
    else:
        acc, gates = refs
    x = pl.program_id(0)

    @pl.when(x == 0)
    def _():
        acc[...] = acc_in[...] if flip else jnp.zeros(acc.shape, F32)
        gates[...] = gate_in[...] if flip else jnp.zeros(gates.shape, F32)

    g = piece[0]
    scaled = (g.astype(F32) * gate[...]).astype(BF16)
    acc[...] += dot_nt(w[...], scaled)
    terms = dot_nn(ot[...], g) * w[...].astype(F32)
    row = jnp.sum(terms, axis=0, keepdims=True)
    count = g.shape[1] // 128
    block = piece_block(info, flip, ys, xs, x)
    for i in range(count):
        gates[pl.ds(block * count + i, 1), :] = row[:, i * 128 : (i + 1) * 128]
    if not flip:
        return

    @pl.when(x == xs - 1)
    def _():
        tile = ot.shape[1]
        rounded = acc[...].astype(BF16)
        dot_out[...] = rounded
        prod = rounded.astype(F32) * ot[...].astype(F32)
        for h in range(ot.shape[0] // HEAD_DIM):
            d = jnp.sum(prod[h * HEAD_DIM : (h + 1) * HEAD_DIM, :], axis=0, keepdims=True)
            delta_out[8 * h : 8 * h + 8, :] = jnp.broadcast_to(d, (8, tile))
        for i in range(gate_out.shape[0]):
            gate_out[i] = gates[...]


def proj_call(flip, sizes, info, w, gate, ot, pieces, carried=()):
    ys, xs = sizes[3:]
    width, tile = ot.shape
    heads = width // HEAD_DIM
    cols = pieces.shape[2]
    rows = w.shape[1] // 128
    acc = jax.ShapeDtypeStruct((width, tile), F32)
    gates = jax.ShapeDtypeStruct((rows, 128), F32)
    if flip:
        out_shape = [
            jax.ShapeDtypeStruct((width, tile), BF16),
            jax.ShapeDtypeStruct((8 * heads, tile), F32),
            jax.ShapeDtypeStruct((ys * xs, rows, 128), F32),
        ]
        scratch = [pltpu.VMEM((width, tile), F32), pltpu.VMEM((rows, 128), F32)]
    else:
        out_shape = [acc, gates]
        scratch = []

    def column(x, info_ref):
        return (0, piece_block(info_ref, flip, ys, xs, x))

    return pl.pallas_call(
        functools.partial(proj_kernel, flip, ys, xs),
        grid_spec=pltpu.PrefetchScalarGridSpec(
            num_scalar_prefetch=1,
            grid=(xs,),
            in_specs=[
                pl.BlockSpec((width, cols), column),
                pl.BlockSpec((1, cols), column),
                whole((width, tile)),
                pl.BlockSpec((1, tile, cols), lambda x, _: (x, 0, 0)),
            ]
            + [whole(c.shape) for c in carried],
            out_specs=[whole(o.shape) for o in out_shape],
            scratch_shapes=scratch,
        ),
        out_shape=out_shape,
        compiler_params=params("arbitrary"),
        cost_estimate=pl.CostEstimate(
            flops=4 * tile * width * cols * xs,
            bytes_accessed=2 * (tile + width) * cols * xs,
            transcendentals=0,
        ),
        name="proj",
    )(info, w, gate, ot, pieces, *carried)


def bwd_math(keys, values, q, dot, lse, delta, dq, extra):
    s = dot_nt(keys, q[...]) * C1
    if extra is not None:
        s = s + extra
    p = jnp.exp2(s - lse[0:1, :])
    dp = dot_nn(values, dot[...])
    ds = (p * (dp - delta[0:1, :])).astype(BF16)
    dv = dot_nt(p.astype(BF16), dot[...])
    dk = dot_nn(ds, q[...]) * SCALE
    dq[...] += dot_tn(keys, ds)
    return dk, dv


def bwd_block(info, h, a, b, block, out, q, dot, lse, delta, dq):
    def run():
        dk, dv = bwd_math(block[0], block[1], q, dot, lse, delta, dq, None)
        out[0] = dk.astype(out.dtype)
        out[1] = dv.astype(out.dtype)

    if (a, b) == (0, 0):
        run()
    else:
        ok = open_block(info, h, a, b)
        pl.when(ok)(run)

        @pl.when(jnp.logical_not(ok))
        def _():
            out[...] = jnp.zeros(out.shape, out.dtype)


def bwd_side_kernel(
    info, q, dot, lse, delta, tk, tv, mask, left, right, left_out, right_out, text_out, dq_out
):
    h = pl.program_id(0)
    dq_out[...] = jnp.zeros(dq_out.shape, F32)
    dk, dv = bwd_math(tk[...], tv[...], q, dot, lse, delta, dq_out, mask_column(mask))
    text_out[0] = dk.astype(BF16)
    text_out[1] = dv.astype(BF16)
    for b, ref, out in ((-1, left, left_out), (1, right, right_out)):
        for a in (-1, 0, 1):
            bwd_block(
                info, h, a, b, ref.at[a + 1], out.at[a + 1], q, dot, lse, delta, dq_out
            )


def bwd_near_kernel(
    info, q, dot, lse, delta, dq_in, cos, sin, up, own, down, up_out, own_out, down_out, gq_out, dq
):
    h = pl.program_id(0)
    dq[...] = dq_in[...]
    for a, ref, out in ((-1, up, up_out), (1, down, down_out), (0, own, own_out)):
        bwd_block(info, h, a, 0, ref, out, q, dot, lse, delta, dq)
    x = jnp.transpose(dq[...]) * SCALE
    lane = lax.broadcasted_iota(jnp.int32, x.shape, 1)
    gq_out[...] = (x * cos[...] - partner(x, lane) * sin[...]).astype(BF16)


def bwd_specs(tile):
    return [
        smem(),
        pl.BlockSpec((tile, HEAD_DIM), lambda h: (0, h)),
        pl.BlockSpec((HEAD_DIM, tile), lambda h: (h, 0)),
        pl.BlockSpec((8, tile), lambda h: (h, 0)),
        pl.BlockSpec((8, tile), lambda h: (h, 0)),
    ]


def bwd_cost(tile, keys, width):
    return pl.CostEstimate(
        flops=10 * tile * keys * width, bytes_accessed=8 * keys * width, transcendentals=0
    )


def bwd_side_call(common, text_keys, text_values, mask, left, right):
    info, q, dot, lse, delta = common
    tile, width = q.shape
    txt = text_keys.shape[0]
    stack = jax.ShapeDtypeStruct((3, 2, tile, width), BF16)
    return pl.pallas_call(
        bwd_side_kernel,
        grid=(width // HEAD_DIM,),
        in_specs=bwd_specs(tile)
        + [half_spec(txt), half_spec(txt), whole((1, txt))]
        + [stack_spec(tile)] * 2,
        out_specs=[stack_spec(tile)] * 2 + [kv_spec(txt), row_spec(HEAD_DIM, tile)],
        out_shape=[
            stack,
            stack,
            jax.ShapeDtypeStruct((2, txt, width), BF16),
            jax.ShapeDtypeStruct((width, tile), F32),
        ],
        compiler_params=params("arbitrary"),
        cost_estimate=bwd_cost(tile, 6 * tile + txt, width),
        name="bwd_side",
    )(info, q, dot, lse, delta, text_keys, text_values, mask, left, right)


def bwd_near_call(common, dq, cos, sin, up, own, down):
    info, q, dot, lse, delta = common
    tile, width = q.shape
    table = whole((tile, HEAD_DIM))
    part = jax.ShapeDtypeStruct((2, tile, width), F32)
    return pl.pallas_call(
        bwd_near_kernel,
        grid=(width // HEAD_DIM,),
        in_specs=bwd_specs(tile)
        + [row_spec(HEAD_DIM, tile), table, table]
        + [kv_spec(tile)] * 3,
        out_specs=[kv_spec(tile)] * 3 + [half_spec(tile)],
        out_shape=[part, part, part, jax.ShapeDtypeStruct((tile, width), BF16)],
        scratch_shapes=[pltpu.VMEM((HEAD_DIM, tile), F32)],
        compiler_params=params("arbitrary"),
        cost_estimate=bwd_cost(tile, 3 * tile, width),
        name="bwd_near",
    )(info, q, dot, lse, delta, dq, cos, sin, up, own, down)


def pair_sum_kernel(up, down, left, right, up_out, down_out):
    for i, part, out in ((0, up, up_out), (2, down, down_out)):
        out[...] = (part[...] + left[i].astype(F32) + right[i].astype(F32)).astype(BF16)


def pair_sum_call(up, down, left, right):
    tile, width = up.shape[1:]
    shape = jax.ShapeDtypeStruct((2, tile, width), BF16)
    return pl.pallas_call(
        pair_sum_kernel,
        grid=(width // HEAD_DIM,),
        in_specs=[kv_spec(tile)] * 2 + [stack_spec(tile)] * 2,
        out_specs=[kv_spec(tile)] * 2,
        out_shape=[shape] * 2,
        compiler_params=params("arbitrary"),
        name="pair_sum",
    )(up, down, left, right)


def finish_kernel(own, left, right, up, down, cos, sin, gk_out, gv_out):
    total = own[...]
    for other in (left[0], right[0], up[...], down[...]):
        total = total + other.astype(F32)
    x = total[0]
    lane = lax.broadcasted_iota(jnp.int32, x.shape, 1)
    gk_out[...] = (x * cos[...] - partner(x, lane) * sin[...]).astype(BF16)
    gv_out[...] = total[1].astype(BF16)


def finish_call(own, left, right, up, down, cos, sin):
    tile, width = own.shape[1:]
    table = whole((tile, HEAD_DIM))
    middle = pl.BlockSpec((1, 2, tile, HEAD_DIM), lambda h: (1, 0, 0, h))
    shape = jax.ShapeDtypeStruct((tile, width), BF16)
    return pl.pallas_call(
        finish_kernel,
        grid=(width // HEAD_DIM,),
        in_specs=[kv_spec(tile), middle, middle, kv_spec(tile), kv_spec(tile), table, table],
        out_specs=[half_spec(tile)] * 2,
        out_shape=[shape, shape],
        compiler_params=params("arbitrary", limit=SMALL),
        name="finish",
    )(own, left, right, up, down, cos, sin)


def split_pair(values):
    hi = values.astype(BF16)
    return hi, (values - hi.astype(F32)).astype(BF16)


def pack_kernel(text, gate, out):
    groups, rows, _ = out.shape
    width = text.shape[1]
    out[:, :, :width] = text[...].reshape(groups, rows, width)
    out[:, :, width:] = jnp.zeros((groups, rows, 128), BF16)
    hi, lo = split_pair(jnp.sum(gate[...], axis=0))
    for i in range(gate.shape[1]):
        out[i, 0:1, width:] = hi[i : i + 1, :]
        out[i, 1:2, width:] = lo[i : i + 1, :]


def pack_call(text, gate, groups):
    rows = text.shape[0] // groups
    return pl.pallas_call(
        pack_kernel,
        in_specs=[pl.BlockSpec(memory_space=pltpu.VMEM)] * 2,
        out_specs=pl.BlockSpec(memory_space=pltpu.VMEM),
        out_shape=jax.ShapeDtypeStruct((groups, rows, text.shape[1] + 128), BF16),
        compiler_params=params(limit=SMALL),
        name="pack",
    )(text, gate)


def chunk_sum_kernel(width, got, out):
    total = jnp.sum(got[...].astype(F32), axis=0)
    text = total[:, :width].astype(BF16)
    hi, lo = split_pair(total[0:1, width:] + total[1:2, width:])
    row = lax.broadcasted_iota(jnp.int32, (total.shape[0], 128), 0)
    side = jnp.where(
        row == 0, hi.astype(F32), jnp.where(row == 1, lo.astype(F32), 0.0)
    ).astype(BF16)
    groups = out.shape[0]
    out[:, :, :width] = jnp.broadcast_to(text[None], (groups, *text.shape))
    out[:, :, width:] = jnp.broadcast_to(side[None], (groups, *side.shape))


def chunk_sum_call(got, width):
    return pl.pallas_call(
        functools.partial(chunk_sum_kernel, width),
        in_specs=[pl.BlockSpec(memory_space=pltpu.VMEM)],
        out_specs=pl.BlockSpec(memory_space=pltpu.VMEM),
        out_shape=jax.ShapeDtypeStruct(got.shape, BF16),
        compiler_params=params(limit=SMALL),
        name="chunk_sum",
    )(got)


def unpack_kernel(got, keys_out, values_out, gate_out):
    groups, rows, _ = got.shape
    width = keys_out.shape[1]
    half = groups // 2
    keys_out[...] = got[:half, :, :width].reshape(half * rows, width)
    values_out[...] = got[half:, :, :width].reshape(half * rows, width)
    for i in range(gate_out.shape[0]):
        pair = got[i, :, width:].astype(F32)
        gate_out[i : i + 1, :] = pair[0:1, :] + pair[1:2, :]


def unpack_call(got, width, gate_rows):
    groups, rows, _ = got.shape
    text = jax.ShapeDtypeStruct((groups // 2 * rows, width), BF16)
    return pl.pallas_call(
        unpack_kernel,
        in_specs=[pl.BlockSpec(memory_space=pltpu.VMEM)],
        out_specs=[pl.BlockSpec(memory_space=pltpu.VMEM)] * 3,
        out_shape=[text, text, jax.ShapeDtypeStruct((gate_rows, 128), F32)],
        compiler_params=params(limit=SMALL),
        name="unpack",
    )(got)


def shift(array, axis, by, wrap=False):
    length = lax.axis_size(axis)
    pairs = [(i, (i + by) % length) for i in range(length) if wrap or 0 <= i + by < length]
    return lax.ppermute(array, axis, pairs)


def swap(array, axis, bit):
    length = lax.axis_size(axis)
    return lax.ppermute(array, axis, [(i, i ^ bit) for i in range(length)])


def spread(array, axis):
    copies = jnp.broadcast_to(array[None], (lax.axis_size(axis), *array.shape))
    return lax.all_to_all(copies, axis, 0, 0, tiled=True)


def on_device(
    query_in,
    key_in,
    value_in,
    text_keys,
    text_values,
    text_mask,
    window_reach,
    tile_map,
    out_weight,
    gate_scale,
    grad_out,
):
    _, width = query_in.shape
    seq_count = lax.axis_size(SEQ)
    sizes = tuple(lax.axis_size(axis) for axis in (*SEQ, *HEAD))
    mask = text_mask.reshape(1, -1)

    g_y = swap(grad_out, "yhi", 1)
    g_x = spread(grad_out, "x")

    q, kv, cos, sin, info = rotate_call(sizes, window_reach, tile_map, query_in, key_in, value_in)

    kv_up, kv_down = shift(kv, "z", 1), shift(kv, "z", -1)
    stack = stack_call(kv_up, kv, kv_down)
    kv_left, kv_right = shift(stack, COL, 1), shift(stack, COL, -1)
    gy_x = spread(g_y, "x")

    partial = fwd_near_call(info, q, kv, kv_up, kv_down, text_keys, text_values, mask)
    ot, lse = fwd_side_call(info, q, kv_left, kv_right, *partial)

    gate = gate_scale.reshape(1, -1)
    carried = proj_call(False, sizes, info, out_weight, gate, ot, g_x)
    dot, delta, gate_terms = proj_call(
        True, sizes, info, out_weight, gate, ot, gy_x, carried
    )
    gate_terms = lax.all_to_all(gate_terms, HEAD, 0, 0, tiled=True)

    common = (info, q, dot, lse, delta)
    left, right, text_part, dq = bwd_side_call(
        common, text_keys, text_values, mask, kv_left, kv_right
    )
    back_left = shift(left, COL, -1)
    back_right = shift(right, COL, 1)
    packed = pack_call(text_part.reshape(-1, width), gate_terms, seq_count)
    got = lax.all_to_all(packed, SEQ, 0, 0, tiled=True)
    up, own, down, grad_query = bwd_near_call(common, dq, cos, sin, kv_up, kv, kv_down)

    up, down = pair_sum_call(up, down, back_left, back_right)
    up = shift(up, "z", -1)
    down = shift(down, "z", 1)

    chunk = chunk_sum_call(got, width)
    summed = lax.all_to_all(chunk, SEQ, 0, 0, tiled=True)
    grad_text_keys, grad_text_values, grad_gate = unpack_call(
        summed, width, out_weight.shape[1] // 128
    )
    grad_key, grad_value = finish_call(own, back_left, back_right, up, down, cos, sin)
    return (
        grad_query,
        grad_key,
        grad_value,
        grad_text_keys,
        grad_text_values,
        grad_gate.reshape(-1),
    )


def solution(mesh):
    fine = Mesh(mesh.devices.reshape(SIZES), (*SEQ, *HEAD))
    head = P(SEQ, HEAD)
    placed = (
        head,
        head,
        head,
        P(None, HEAD),
        P(None, HEAD),
        P(),
        P(HEAD, None),
        P(),
        P(HEAD, None),
        P(),
        head,
    )

    return jax.shard_map(
        on_device,
        mesh=fine,
        in_specs=placed,
        out_specs=(head, head, head, P(None, HEAD), P(None, HEAD), P()),
        check_vma=False,
    )


SIZES = (8, 4, 2, 2, 4)
```

```python
import functools
import math

import jax
import jax.numpy as jnp
import numpy as np
from jax import lax
from jax.experimental import pallas as pl
from jax.experimental.pallas import tpu as pltpu
from jax.sharding import Mesh
from jax.sharding import PartitionSpec as P


HEAD_DIM = 128
TILE_H = 8
TILE_W = 8
SECTIONS = ((0, 16), (16, 56), (72, 56))
THETA = 256.0
SCALE = HEAD_DIM ** -0.5
LOG2E = math.log2(math.e)
C1 = SCALE * LOG2E
SEQ = ("z", "y", "core")
COL = ("y", "core")
CHIPS = ("z", "y")
HEAD = ("yhi", "x")
F32 = jnp.float32
BF16 = jnp.bfloat16
NEG = -1e30
VMEM_LIMIT = 66_000_000
SMALL = 16_000_000


def dot_nn(a, b):
    return lax.dot_general(a, b, (((1,), (0,)), ((), ())), preferred_element_type=F32)


def dot_nt(a, b):
    return lax.dot_general(a, b, (((1,), (1,)), ((), ())), preferred_element_type=F32)


def dot_tn(a, b):
    return lax.dot_general(a, b, (((0,), (0,)), ((), ())), preferred_element_type=F32)


def params(*semantics, limit=VMEM_LIMIT):
    return pltpu.CompilerParams(
        dimension_semantics=semantics or None, vmem_limit_bytes=limit
    )


def lane_freqs():
    freqs = np.zeros((8, HEAD_DIM), np.float32)
    for offset, length in SECTIONS:
        half = length // 2
        f = np.float32(THETA) ** (
            np.float32(-2.0) * np.arange(half, dtype=np.float32) / np.float32(length)
        )
        freqs[:, offset : offset + half] = f
        freqs[:, offset + half : offset + length] = f
    return freqs


def partner(x, lane):
    near = jnp.where(lane < 8, pltpu.roll(x, HEAD_DIM - 8, 1), pltpu.roll(x, 8, 1))
    first = ((lane >= 16) & (lane < 44)) | ((lane >= 72) & (lane < 100))
    far = jnp.where(first, pltpu.roll(x, HEAD_DIM - 28, 1), pltpu.roll(x, 28, 1))
    return jnp.where(lane < 16, near, far)


def whole(shape):
    return pl.BlockSpec(shape, lambda *_: (0,) * len(shape))


def smem():
    return pl.BlockSpec(memory_space=pltpu.SMEM)


def rot_kernel(sizes, reach, tiles, freq, q, k, v, q_out, kv_out, cos_out, sin_out, info):
    tile = q.shape[0]

    @pl.when(pl.program_id(0) == 0)
    def _():
        rows, ys, cores, _, _ = sizes
        row = lax.axis_index("z")
        col = lax.axis_index("y") * cores + lax.axis_index("core")
        info[0] = row
        info[1] = col
        info[2] = rows
        info[3] = ys * cores
        info[4] = lax.axis_index("yhi")
        info[5] = lax.axis_index("core")
        for h in range(reach.shape[0]):
            info[8 + 2 * h] = reach[h, 0]
            info[9 + 2 * h] = reach[h, 1]
        own = row * (ys * cores) + col
        frames = tile // (TILE_H * TILE_W)
        step = lax.broadcasted_iota(jnp.int32, (8, HEAD_DIM), 0)
        lane = lax.broadcasted_iota(jnp.int32, (8, HEAD_DIM), 1)
        first = (
            (lane < 8) | ((lane >= 16) & (lane < 44)) | ((lane >= 72) & (lane < 100))
        )
        f = freq[...]

        def table(base):
            angle = (base + step).astype(F32) * f
            s = jnp.sin(angle)
            return jnp.cos(angle), jnp.where(first, -s, s)

        cf, sf = table(tiles[0, own] * frames)
        cr, sr = table(tiles[1, own] * TILE_H)
        cc, sc = table(tiles[2, own] * TILE_W)
        for r in range(TILE_H):
            crr = jnp.where(lane < 72, cr[r : r + 1, :], cc)
            srr = jnp.where(lane < 72, sr[r : r + 1, :], sc)
            for t in range(frames):
                at = (t * TILE_H + r) * TILE_W
                cos_out[at : at + TILE_W, :] = jnp.where(lane < 16, cf[t : t + 1, :], crr)
                sin_out[at : at + TILE_W, :] = jnp.where(lane < 16, sf[t : t + 1, :], srr)

    lane = lax.broadcasted_iota(jnp.int32, (tile, HEAD_DIM), 1)
    cos, sin = cos_out[...], sin_out[...]
    for source, target in ((q, q_out), (k, kv_out.at[0])):
        x = source[...].astype(F32)
        target[...] = (x * cos + partner(x, lane) * sin).astype(BF16)
    kv_out[1] = v[...]


def rotate_call(sizes, reach, tile_map, q_in, k_in, v_in):
    tile, width = q_in.shape
    heads = width // HEAD_DIM
    half = pl.BlockSpec((tile, HEAD_DIM), lambda h: (0, h))
    table = whole((tile, HEAD_DIM))
    return pl.pallas_call(
        functools.partial(rot_kernel, sizes),
        grid=(heads,),
        in_specs=[smem(), smem(), whole((8, HEAD_DIM)), half, half, half],
        out_specs=[half, kv_spec(tile), table, table, smem()],
        out_shape=[
            jax.ShapeDtypeStruct((tile, width), BF16),
            jax.ShapeDtypeStruct((2, tile, width), BF16),
            jax.ShapeDtypeStruct((tile, HEAD_DIM), F32),
            jax.ShapeDtypeStruct((tile, HEAD_DIM), F32),
            jax.ShapeDtypeStruct((24,), jnp.int32),
        ],
        compiler_params=params("arbitrary"),
        name="rot",
    )(reach, tile_map.T, jnp.asarray(lane_freqs()), q_in, k_in, v_in)


def open_block(info, h, a, b):
    ok = (info[8 + 2 * h] >= abs(a)) & (info[9 + 2 * h] >= abs(b))
    if a:
        row = info[0] + a
        ok = ok & (row >= 0) & (row < info[2])
    if b:
        col = info[1] + b
        ok = ok & (col >= 0) & (col < info[3])
    return ok


def mask_column(mask):
    closed = jnp.where(mask[...] == 1, 0.0, NEG).astype(F32)
    return jnp.transpose(jnp.broadcast_to(closed, (8, closed.shape[1])))[:, 0:1]


def fwd_block(keys, values, extra, q, m, l, acc):
    s = dot_nt(keys, q[...]) * C1
    if extra is not None:
        s = s + extra
    m_old = m[0:1, :]
    m_new = jnp.maximum(m_old, jnp.max(s, axis=0, keepdims=True))
    p = jnp.exp2(s - m_new)
    alpha = jnp.exp2(m_old - m_new)
    m[0:1, :] = m_new
    l[0:1, :] = l[0:1, :] * alpha + jnp.sum(p, axis=0, keepdims=True)
    acc[...] = acc[...] * alpha + dot_tn(values, p.astype(BF16))


def fwd_near_kernel(info, q, own, up, down, tk, tv, mask, acc, m, l):
    h = pl.program_id(0)
    m[...] = jnp.full(m.shape, NEG, F32)
    l[...] = jnp.zeros(l.shape, F32)
    acc[...] = jnp.zeros(acc.shape, F32)
    fwd_block(own[0], own[1], None, q, m, l, acc)
    fwd_block(tk[...], tv[...], mask_column(mask), q, m, l, acc)
    for a, ref in ((-1, up), (1, down)):

        @pl.when(open_block(info, h, a, 0))
        def _(ref=ref):
            fwd_block(ref[0], ref[1], None, q, m, l, acc)


def fwd_side_kernel(
    info, q, left, right, acc_in, m_in, l_in, dot, ot_out, lse_out, delta_out, acc, m, l
):
    h = pl.program_id(0)
    acc[...] = acc_in[...]
    m[...] = m_in[...]
    l[...] = l_in[...]
    for b, ref in ((-1, left), (1, right)):
        for a in (-1, 0, 1):

            @pl.when(open_block(info, h, a, b))
            def _(ref=ref, a=a):
                fwd_block(ref[a + 1, 0], ref[a + 1, 1], None, q, m, l, acc)

    ot = (acc[...] * (1.0 / l[0:1, :])).astype(BF16)
    ot_out[...] = ot
    delta = jnp.sum(ot.astype(F32) * dot[...].astype(F32), axis=0, keepdims=True)
    delta_out[...] = jnp.broadcast_to(delta, delta_out.shape)
    lse_out[...] = jnp.broadcast_to(m[0:1, :] + jnp.log2(l[0:1, :]), lse_out.shape)


def kv_spec(tile):
    return pl.BlockSpec((2, tile, HEAD_DIM), lambda h: (0, 0, h))


def stack_spec(tile):
    return pl.BlockSpec((3, 2, tile, HEAD_DIM), lambda h: (0, 0, 0, h))


def half_spec(rows):
    return pl.BlockSpec((rows, HEAD_DIM), lambda h: (0, h))


def row_spec(rows, tile):
    return pl.BlockSpec((rows, tile), lambda h: (h, 0))


def fwd_near_call(info, q, own, up, down, text_keys, text_values, mask):
    tile, width = q.shape
    heads = width // HEAD_DIM
    txt = text_keys.shape[0]
    keys = 3 * tile + txt
    stats = jax.ShapeDtypeStruct((8 * heads, tile), F32)
    return pl.pallas_call(
        fwd_near_kernel,
        grid=(heads,),
        in_specs=[smem(), half_spec(tile)]
        + [kv_spec(tile)] * 3
        + [half_spec(txt), half_spec(txt), whole((1, txt))],
        out_specs=[row_spec(HEAD_DIM, tile), row_spec(8, tile), row_spec(8, tile)],
        out_shape=[jax.ShapeDtypeStruct((width, tile), F32), stats, stats],
        compiler_params=params("arbitrary"),
        cost_estimate=pl.CostEstimate(
            flops=4 * tile * keys * width, bytes_accessed=4 * keys * width, transcendentals=0
        ),
        name="fwd_near",
    )(info, q, own, up, down, text_keys, text_values, mask)


def fwd_side_call(info, q, left, right, acc, m, l, dot):
    tile, width = q.shape
    heads = width // HEAD_DIM
    keys = 6 * tile
    return pl.pallas_call(
        fwd_side_kernel,
        grid=(heads,),
        in_specs=[
            smem(),
            half_spec(tile),
            stack_spec(tile),
            stack_spec(tile),
            row_spec(HEAD_DIM, tile),
            row_spec(8, tile),
            row_spec(8, tile),
            row_spec(HEAD_DIM, tile),
        ],
        out_specs=[row_spec(HEAD_DIM, tile), row_spec(8, tile), row_spec(8, tile)],
        out_shape=[
            jax.ShapeDtypeStruct((width, tile), BF16),
            jax.ShapeDtypeStruct((8 * heads, tile), F32),
            jax.ShapeDtypeStruct((8 * heads, tile), F32),
        ],
        scratch_shapes=[
            pltpu.VMEM((HEAD_DIM, tile), F32),
            pltpu.VMEM((8, tile), F32),
            pltpu.VMEM((8, tile), F32),
        ],
        compiler_params=params("arbitrary"),
        cost_estimate=pl.CostEstimate(
            flops=4 * tile * keys * width, bytes_accessed=4 * keys * width, transcendentals=0
        ),
        name="fwd_side",
    )(info, q, left, right, acc, m, l, dot)


def stack_kernel(up, own, down, out):
    out[0] = up[...]
    out[1] = own[...]
    out[2] = down[...]


def stack_call(up, own, down):
    tile, width = own.shape[1:]
    return pl.pallas_call(
        stack_kernel,
        grid=(width // HEAD_DIM,),
        in_specs=[kv_spec(tile)] * 3,
        out_specs=stack_spec(tile),
        out_shape=jax.ShapeDtypeStruct((3, 2, tile, width), BF16),
        compiler_params=params("arbitrary", limit=SMALL),
        name="stack",
    )(up, own, down)


def first_block(info, flip, ys, xs):
    return (ys - 1 - info[4] if flip else info[4]) * xs


def fetch(w, pieces, w_buf, p_buf, sems, slot, block):
    cols = p_buf.shape[2]
    at = pl.multiple_of(block * cols, 128)
    copies = [
        pltpu.make_async_copy(pieces, p_buf.at[slot], sems.at[2 * slot]),
        pltpu.make_async_copy(
            w.at[:, pl.ds(at, cols)], w_buf.at[slot], sems.at[2 * slot + 1]
        ),
    ]
    for copy in copies:
        copy.start()
    return copies


def proj_kernel(flip, ys, xs, info, w, gate, pieces, *refs):
    *acc_in, out, w_buf, p_buf, sems = refs
    start = first_block(info, flip, ys, xs)
    copies = [
        fetch(w, pieces.at[x], w_buf, p_buf, sems, x, start + x) for x in range(xs)
    ]
    cols = p_buf.shape[2]
    acc = acc_in[0][...] if acc_in else None
    for x in range(xs):
        for copy in copies[x]:
            copy.wait()
        at = pl.multiple_of((start + x) * cols, 128)
        scaled = (p_buf[x].astype(F32) * gate[:, pl.ds(at, cols)]).astype(BF16)
        part = dot_nt(w_buf[x], scaled)
        acc = part if acc is None else acc + part
    out[...] = acc.astype(out.dtype)


def proj_call(flip, sizes, info, w, gate, pieces, *acc):
    ys, xs = sizes[3:]
    width = w.shape[0]
    _, tile, cols = pieces.shape
    vmem = pl.BlockSpec(memory_space=pltpu.VMEM)
    hbm = pl.BlockSpec(memory_space=pltpu.HBM)
    return pl.pallas_call(
        functools.partial(proj_kernel, flip, ys, xs),
        in_specs=[smem(), hbm, vmem, hbm] + [vmem] * len(acc),
        out_specs=vmem,
        out_shape=jax.ShapeDtypeStruct((width, tile), BF16 if flip else F32),
        scratch_shapes=[
            pltpu.VMEM((xs, width, cols), BF16),
            pltpu.VMEM((xs, tile, cols), BF16),
            pltpu.SemaphoreType.DMA((2 * xs,)),
        ],
        compiler_params=params(),
        cost_estimate=pl.CostEstimate(
            flops=2 * tile * width * cols * xs,
            bytes_accessed=2 * (tile + width) * cols * xs,
            transcendentals=0,
        ),
        name="proj",
    )(info, w, gate, pieces, *acc)


def gate_kernel(ys, xs, info, w, ot, near, far, out, w_buf, p_buf, sems, gates):
    jobs = []
    for flip, pieces in ((False, near), (True, far)):
        start = first_block(info, flip, ys, xs)
        for x in range(xs):
            slot = len(jobs)
            copies = fetch(w, pieces.at[x], w_buf, p_buf, sems, slot, start + x)
            jobs.append((slot, start + x, copies))
    count = p_buf.shape[2] // 128
    for slot, block, copies in jobs:
        for copy in copies:
            copy.wait()
        terms = dot_nn(ot[...], p_buf[slot]) * w_buf[slot].astype(F32)
        row = jnp.sum(terms, axis=0, keepdims=True)
        for i in range(count):
            gates[pl.ds(block * count + i, 1), :] = row[:, i * 128 : (i + 1) * 128]
    for i in range(out.shape[0]):
        out[i] = gates[...]


def gate_call(sizes, info, w, ot, near, far):
    ys, xs = sizes[3:]
    width, tile = ot.shape
    cols = near.shape[2]
    rows = w.shape[1] // 128
    vmem = pl.BlockSpec(memory_space=pltpu.VMEM)
    hbm = pl.BlockSpec(memory_space=pltpu.HBM)
    return pl.pallas_call(
        functools.partial(gate_kernel, ys, xs),
        in_specs=[smem(), hbm, vmem, hbm, hbm],
        out_specs=vmem,
        out_shape=jax.ShapeDtypeStruct((sizes[2] * ys * xs, rows, 128), F32),
        scratch_shapes=[
            pltpu.VMEM((ys * xs, width, cols), BF16),
            pltpu.VMEM((ys * xs, tile, cols), BF16),
            pltpu.SemaphoreType.DMA((2 * ys * xs,)),
            pltpu.VMEM((rows, 128), F32),
        ],
        compiler_params=params(),
        cost_estimate=pl.CostEstimate(
            flops=2 * tile * w.size, bytes_accessed=2 * w.size, transcendentals=0
        ),
        name="gate_terms",
    )(info, w, ot, near, far)


def bwd_math(keys, values, q, dot, lse, delta, dq, extra):
    s = dot_nt(keys, q[...]) * C1
    if extra is not None:
        s = s + extra
    p = jnp.exp2(s - lse[0:1, :])
    dp = dot_nn(values, dot[...])
    ds = (p * (dp - delta[0:1, :])).astype(BF16)
    dv = dot_nt(p.astype(BF16), dot[...])
    dk = dot_nn(ds, q[...]) * SCALE
    dq[...] += dot_tn(keys, ds)
    return dk, dv


def bwd_block(info, h, a, b, block, out, q, dot, lse, delta, dq):
    def run():
        dk, dv = bwd_math(block[0], block[1], q, dot, lse, delta, dq, None)
        out[0] = dk.astype(out.dtype)
        out[1] = dv.astype(out.dtype)

    if (a, b) == (0, 0):
        run()
    else:
        ok = open_block(info, h, a, b)
        pl.when(ok)(run)

        @pl.when(jnp.logical_not(ok))
        def _():
            out[...] = jnp.zeros(out.shape, out.dtype)


def bwd_side_kernel(
    info, q, dot, lse, delta, tk, tv, mask, left, right, left_out, right_out, keep, give, dq_out
):
    h = pl.program_id(0)
    dq_out[...] = jnp.zeros(dq_out.shape, F32)
    dk, dv = bwd_math(tk[...], tv[...], q, dot, lse, delta, dq_out, mask_column(mask))
    first = info[5] == 0
    keep[...] = jnp.where(first, dk, dv)
    give[...] = jnp.where(first, dv, dk).astype(BF16)
    for b, ref, out in ((-1, left, left_out), (1, right, right_out)):
        for a in (-1, 0, 1):
            bwd_block(
                info, h, a, b, ref.at[a + 1], out.at[a + 1], q, dot, lse, delta, dq_out
            )


def bwd_near_kernel(
    info, q, dot, lse, delta, dq_in, cos, sin, up, own, down, up_out, own_out, down_out, gq_out, dq
):
    h = pl.program_id(0)
    dq[...] = dq_in[...]
    for a, ref, out in ((-1, up, up_out), (1, down, down_out), (0, own, own_out)):
        bwd_block(info, h, a, 0, ref, out, q, dot, lse, delta, dq)
    x = jnp.transpose(dq[...]) * SCALE
    lane = lax.broadcasted_iota(jnp.int32, x.shape, 1)
    gq_out[...] = (x * cos[...] - partner(x, lane) * sin[...]).astype(BF16)


def bwd_specs(tile):
    return [
        smem(),
        pl.BlockSpec((tile, HEAD_DIM), lambda h: (0, h)),
        pl.BlockSpec((HEAD_DIM, tile), lambda h: (h, 0)),
        pl.BlockSpec((8, tile), lambda h: (h, 0)),
        pl.BlockSpec((8, tile), lambda h: (h, 0)),
    ]


def bwd_cost(tile, keys, width):
    return pl.CostEstimate(
        flops=10 * tile * keys * width, bytes_accessed=8 * keys * width, transcendentals=0
    )


def bwd_side_call(common, text_keys, text_values, mask, left, right):
    info, q, dot, lse, delta = common
    tile, width = q.shape
    txt = text_keys.shape[0]
    stack = jax.ShapeDtypeStruct((3, 2, tile, width), BF16)
    return pl.pallas_call(
        bwd_side_kernel,
        grid=(width // HEAD_DIM,),
        in_specs=bwd_specs(tile)
        + [half_spec(txt), half_spec(txt), whole((1, txt))]
        + [stack_spec(tile)] * 2,
        out_specs=[stack_spec(tile)] * 2
        + [half_spec(txt), half_spec(txt), row_spec(HEAD_DIM, tile)],
        out_shape=[
            stack,
            stack,
            jax.ShapeDtypeStruct((txt, width), F32),
            jax.ShapeDtypeStruct((txt, width), BF16),
            jax.ShapeDtypeStruct((width, tile), F32),
        ],
        compiler_params=params("arbitrary"),
        cost_estimate=bwd_cost(tile, 6 * tile + txt, width),
        name="bwd_side",
    )(info, q, dot, lse, delta, text_keys, text_values, mask, left, right)


def bwd_near_call(common, dq, cos, sin, up, own, down):
    info, q, dot, lse, delta = common
    tile, width = q.shape
    table = whole((tile, HEAD_DIM))
    return pl.pallas_call(
        bwd_near_kernel,
        grid=(width // HEAD_DIM,),
        in_specs=bwd_specs(tile)
        + [row_spec(HEAD_DIM, tile), table, table]
        + [kv_spec(tile)] * 3,
        out_specs=[kv_spec(tile)] * 3 + [half_spec(tile)],
        out_shape=[
            jax.ShapeDtypeStruct((2, tile, width), BF16),
            jax.ShapeDtypeStruct((2, tile, width), F32),
            jax.ShapeDtypeStruct((2, tile, width), BF16),
            jax.ShapeDtypeStruct((tile, width), BF16),
        ],
        scratch_shapes=[pltpu.VMEM((HEAD_DIM, tile), F32)],
        compiler_params=params("arbitrary"),
        cost_estimate=bwd_cost(tile, 3 * tile, width),
        name="bwd_near",
    )(info, q, dot, lse, delta, dq, cos, sin, up, own, down)


def pair_sum_kernel(up, down, up_l, up_r, down_l, down_r, up_out, down_out):
    for part, left, right, out in (
        (up, up_l, up_r, up_out),
        (down, down_l, down_r, down_out),
    ):
        total = part[...].astype(F32) + left[0].astype(F32) + right[0].astype(F32)
        out[...] = total.astype(BF16)


def pair_sum_call(up, down, left, right):
    tile, width = up.shape[1:]
    shape = jax.ShapeDtypeStruct((2, tile, width), BF16)
    top = pl.BlockSpec((1, 2, tile, HEAD_DIM), lambda h: (0, 0, 0, h))
    bottom = pl.BlockSpec((1, 2, tile, HEAD_DIM), lambda h: (2, 0, 0, h))
    return pl.pallas_call(
        pair_sum_kernel,
        grid=(width // HEAD_DIM,),
        in_specs=[kv_spec(tile)] * 2 + [top, top, bottom, bottom],
        out_specs=[kv_spec(tile)] * 2,
        out_shape=[shape] * 2,
        compiler_params=params("arbitrary"),
        name="pair_sum",
    )(up, down, left, right, left, right)


def finish_kernel(own, left, right, up, down, cos, sin, gk_out, gv_out):
    total = own[...]
    for other in (left[0], right[0], up[...], down[...]):
        total = total + other.astype(F32)
    x = total[0]
    lane = lax.broadcasted_iota(jnp.int32, x.shape, 1)
    gk_out[...] = (x * cos[...] - partner(x, lane) * sin[...]).astype(BF16)
    gv_out[...] = total[1].astype(BF16)


def finish_call(own, left, right, up, down, cos, sin):
    tile, width = own.shape[1:]
    table = whole((tile, HEAD_DIM))
    middle = pl.BlockSpec((1, 2, tile, HEAD_DIM), lambda h: (1, 0, 0, h))
    shape = jax.ShapeDtypeStruct((tile, width), BF16)
    return pl.pallas_call(
        finish_kernel,
        grid=(width // HEAD_DIM,),
        in_specs=[kv_spec(tile), middle, middle, kv_spec(tile), kv_spec(tile), table, table],
        out_specs=[half_spec(tile)] * 2,
        out_shape=[shape, shape],
        compiler_params=params("arbitrary", limit=SMALL),
        name="finish",
    )(own, left, right, up, down, cos, sin)


def split_pair(values):
    hi = values.astype(BF16)
    return hi, (values - hi.astype(F32)).astype(BF16)


def pack_kernel(keep, got, gate, out):
    groups, rows, _ = out.shape
    width = keep.shape[1]
    text = (keep[...] + got[...].astype(F32)).astype(BF16)
    out[:, :, :width] = text.reshape(groups, rows, width)
    out[:, :, width:] = jnp.zeros((groups, rows, 128), BF16)
    hi, lo = split_pair(jnp.sum(gate[...], axis=0))
    for i in range(gate.shape[1]):
        out[i, 0:1, width:] = hi[i : i + 1, :]
        out[i, 1:2, width:] = lo[i : i + 1, :]


def pack_call(keep, got, gate, groups):
    txt, width = keep.shape
    return pl.pallas_call(
        pack_kernel,
        in_specs=[pl.BlockSpec(memory_space=pltpu.VMEM)] * 3,
        out_specs=pl.BlockSpec(memory_space=pltpu.VMEM),
        out_shape=jax.ShapeDtypeStruct((groups, txt // groups, width + 128), BF16),
        compiler_params=params(limit=SMALL),
        name="pack",
    )(keep, got, gate)


def chunk_sum_kernel(width, got, out):
    total = jnp.sum(got[...].astype(F32), axis=0)
    text = total[:, :width].astype(BF16)
    hi, lo = split_pair(total[0:1, width:] + total[1:2, width:])
    row = lax.broadcasted_iota(jnp.int32, (total.shape[0], 128), 0)
    side = jnp.where(
        row == 0, hi.astype(F32), jnp.where(row == 1, lo.astype(F32), 0.0)
    ).astype(BF16)
    groups = out.shape[0]
    out[:, :, :width] = jnp.broadcast_to(text[None], (groups, *text.shape))
    out[:, :, width:] = jnp.broadcast_to(side[None], (groups, *side.shape))


def chunk_sum_call(got, width):
    return pl.pallas_call(
        functools.partial(chunk_sum_kernel, width),
        in_specs=[pl.BlockSpec(memory_space=pltpu.VMEM)],
        out_specs=pl.BlockSpec(memory_space=pltpu.VMEM),
        out_shape=jax.ShapeDtypeStruct(got.shape, BF16),
        compiler_params=params(),
        name="chunk_sum",
    )(got)


def unpack_kernel(got, text_out, gate_out):
    groups, rows, _ = got.shape
    width = text_out.shape[1]
    text_out[...] = got[:, :, :width].reshape(groups * rows, width)
    for i in range(gate_out.shape[0]):
        pair = got[i, :, width:].astype(F32)
        gate_out[i : i + 1, :] = pair[0:1, :] + pair[1:2, :]


def unpack_call(got, width, gate_rows):
    groups, rows, _ = got.shape
    vmem = pl.BlockSpec(memory_space=pltpu.VMEM)
    return pl.pallas_call(
        unpack_kernel,
        in_specs=[vmem],
        out_specs=[vmem, vmem],
        out_shape=[
            jax.ShapeDtypeStruct((groups * rows, width), BF16),
            jax.ShapeDtypeStruct((gate_rows, 128), F32),
        ],
        compiler_params=params(limit=SMALL),
        name="unpack",
    )(got)


def choose_kernel(info, own, other, keys_out, values_out):
    first = info[5] == 0
    keys_out[...] = jnp.where(first, own[...], other[...])
    values_out[...] = jnp.where(first, other[...], own[...])


def choose_call(info, own, other):
    vmem = pl.BlockSpec(memory_space=pltpu.VMEM)
    shape = jax.ShapeDtypeStruct(own.shape, BF16)
    return pl.pallas_call(
        choose_kernel,
        in_specs=[smem(), vmem, vmem],
        out_specs=[vmem, vmem],
        out_shape=[shape, shape],
        compiler_params=params(limit=SMALL),
        name="choose",
    )(info, own, other)


def shift(array, axis, by, wrap=False):
    length = lax.axis_size(axis)
    pairs = [(i, (i + by) % length) for i in range(length) if wrap or 0 <= i + by < length]
    return lax.ppermute(array, axis, pairs)


def swap(array, axis, bit):
    length = lax.axis_size(axis)
    return lax.ppermute(array, axis, [(i, i ^ bit) for i in range(length)])


def spread(array, axis):
    copies = jnp.broadcast_to(array[None], (lax.axis_size(axis), *array.shape))
    return lax.all_to_all(copies, axis, 0, 0, tiled=True)


def on_device(
    query_in,
    key_in,
    value_in,
    text_keys,
    text_values,
    text_mask,
    window_reach,
    tile_map,
    out_weight,
    gate_scale,
    grad_out,
):
    _, width = query_in.shape
    sizes = tuple(lax.axis_size(axis) for axis in (*SEQ, *HEAD))
    mask = text_mask.reshape(1, -1)
    gate = gate_scale.reshape(1, -1)

    g_y = swap(grad_out, "yhi", 1)
    g_x = spread(grad_out, "x")

    q, kv, cos, sin, info = rotate_call(
        sizes, window_reach, tile_map, query_in, key_in, value_in
    )

    kv_up, kv_down = shift(kv, "z", 1), shift(kv, "z", -1)
    gy_x = spread(g_y, "x")
    stack = stack_call(kv_up, kv, kv_down)
    kv_left, kv_right = shift(stack, COL, 1), shift(stack, COL, -1)

    partial = fwd_near_call(info, q, kv, kv_up, kv_down, text_keys, text_values, mask)
    acc = proj_call(False, sizes, info, out_weight, gate, g_x)
    dot = proj_call(True, sizes, info, out_weight, gate, gy_x, acc)
    ot, lse, delta = fwd_side_call(info, q, kv_left, kv_right, *partial, dot)

    gate_terms = gate_call(sizes, info, out_weight, ot, g_x, gy_x)
    gate_terms = lax.all_to_all(gate_terms, ("core", *HEAD), 0, 0, tiled=True)

    common = (info, q, dot, lse, delta)
    left, right, keep, give, dq = bwd_side_call(
        common, text_keys, text_values, mask, kv_left, kv_right
    )
    taken = swap(give, "core", 1)
    back_left = shift(left, COL, -1)
    back_right = shift(right, COL, 1)
    packed = pack_call(keep, taken, gate_terms, lax.axis_size(CHIPS))
    got = lax.all_to_all(packed, CHIPS, 0, 0, tiled=True)
    up, own, down, grad_query = bwd_near_call(common, dq, cos, sin, kv_up, kv, kv_down)

    up, down = pair_sum_call(up, down, back_left, back_right)
    up = shift(up, "z", -1)
    down = shift(down, "z", 1)

    chunk = chunk_sum_call(got, width)
    summed = lax.all_to_all(chunk, CHIPS, 0, 0, tiled=True)
    own_text, grad_gate = unpack_call(summed, width, out_weight.shape[1] // 128)
    other_text = swap(own_text, "core", 1)
    grad_key, grad_value = finish_call(own, back_left, back_right, up, down, cos, sin)
    grad_text_keys, grad_text_values = choose_call(info, own_text, other_text)
    return (
        grad_query,
        grad_key,
        grad_value,
        grad_text_keys,
        grad_text_values,
        grad_gate.reshape(-1),
    )


def solution(mesh):
    fine = Mesh(mesh.devices.reshape(SIZES), (*SEQ, *HEAD))
    head = P(SEQ, HEAD)
    placed = (
        head,
        head,
        head,
        P(None, HEAD),
        P(None, HEAD),
        P(),
        P(HEAD, None),
        P(),
        P(HEAD, None),
        P(),
        head,
    )

    return jax.shard_map(
        on_device,
        mesh=fine,
        in_specs=placed,
        out_specs=(head, head, head, P(None, HEAD), P(None, HEAD), P()),
        check_vma=False,
    )


SIZES = (8, 4, 2, 2, 4)
```

```python
import functools
import math

import jax
import jax.numpy as jnp
import numpy as np
from jax import lax
from jax.experimental import pallas as pl
from jax.experimental.pallas import tpu as pltpu
from jax.sharding import Mesh
from jax.sharding import PartitionSpec as P


HEAD_DIM = 128
TILE_H = 8
TILE_W = 8
SECTIONS = ((0, 16), (16, 56), (72, 56))
THETA = 256.0
SCALE = HEAD_DIM ** -0.5
LOG2E = math.log2(math.e)
C1 = SCALE * LOG2E
SEQ = ("z", "y", "core")
COL = ("y", "core")
CHIPS = ("z", "y")
HEAD = ("yhi", "x")
F32 = jnp.float32
BF16 = jnp.bfloat16
NEG = -1e30
VMEM_LIMIT = 66_000_000
SMALL = 16_000_000


def dot_nn(a, b):
    return lax.dot_general(a, b, (((1,), (0,)), ((), ())), preferred_element_type=F32)


def dot_nt(a, b):
    return lax.dot_general(a, b, (((1,), (1,)), ((), ())), preferred_element_type=F32)


def dot_tn(a, b):
    return lax.dot_general(a, b, (((0,), (0,)), ((), ())), preferred_element_type=F32)


def params(*semantics, limit=VMEM_LIMIT):
    return pltpu.CompilerParams(
        dimension_semantics=semantics or None, vmem_limit_bytes=limit
    )


def lane_freqs():
    freqs = np.zeros((8, HEAD_DIM), np.float32)
    for offset, length in SECTIONS:
        half = length // 2
        f = np.float32(THETA) ** (
            np.float32(-2.0) * np.arange(half, dtype=np.float32) / np.float32(length)
        )
        freqs[:, offset : offset + half] = f
        freqs[:, offset + half : offset + length] = f
    return freqs


def partner(x, lane):
    near = jnp.where(lane < 8, pltpu.roll(x, HEAD_DIM - 8, 1), pltpu.roll(x, 8, 1))
    first = ((lane >= 16) & (lane < 44)) | ((lane >= 72) & (lane < 100))
    far = jnp.where(first, pltpu.roll(x, HEAD_DIM - 28, 1), pltpu.roll(x, 28, 1))
    return jnp.where(lane < 16, near, far)


def whole(shape):
    return pl.BlockSpec(shape, lambda *_: (0,) * len(shape))


def smem():
    return pl.BlockSpec(memory_space=pltpu.SMEM)


def rot_kernel(sizes, reach, tiles, freq, q, k, v, q_out, kv_out, cos_out, sin_out, info):
    tile = q.shape[0]

    @pl.when(pl.program_id(0) == 0)
    def _():
        rows, ys, cores, _, _ = sizes
        row = lax.axis_index("z")
        col = lax.axis_index("y") * cores + lax.axis_index("core")
        info[0] = row
        info[1] = col
        info[2] = rows
        info[3] = ys * cores
        info[4] = lax.axis_index("yhi")
        info[5] = lax.axis_index("core")
        for h in range(reach.shape[0]):
            info[8 + 2 * h] = reach[h, 0]
            info[9 + 2 * h] = reach[h, 1]
        own = row * (ys * cores) + col
        frames = tile // (TILE_H * TILE_W)
        step = lax.broadcasted_iota(jnp.int32, (8, HEAD_DIM), 0)
        lane = lax.broadcasted_iota(jnp.int32, (8, HEAD_DIM), 1)
        first = (
            (lane < 8) | ((lane >= 16) & (lane < 44)) | ((lane >= 72) & (lane < 100))
        )
        f = freq[...]

        def table(base):
            angle = (base + step).astype(F32) * f
            s = jnp.sin(angle)
            return jnp.cos(angle), jnp.where(first, -s, s)

        cf, sf = table(tiles[0, own] * frames)
        cr, sr = table(tiles[1, own] * TILE_H)
        cc, sc = table(tiles[2, own] * TILE_W)
        for r in range(TILE_H):
            crr = jnp.where(lane < 72, cr[r : r + 1, :], cc)
            srr = jnp.where(lane < 72, sr[r : r + 1, :], sc)
            for t in range(frames):
                at = (t * TILE_H + r) * TILE_W
                cos_out[at : at + TILE_W, :] = jnp.where(lane < 16, cf[t : t + 1, :], crr)
                sin_out[at : at + TILE_W, :] = jnp.where(lane < 16, sf[t : t + 1, :], srr)

    lane = lax.broadcasted_iota(jnp.int32, (tile, HEAD_DIM), 1)
    cos, sin = cos_out[...], sin_out[...]
    for source, target in ((q, q_out), (k, kv_out.at[0])):
        x = source[...].astype(F32)
        target[...] = (x * cos + partner(x, lane) * sin).astype(BF16)
    kv_out[1] = v[...]


def rotate_call(sizes, reach, tile_map, q_in, k_in, v_in):
    tile, width = q_in.shape
    heads = width // HEAD_DIM
    half = pl.BlockSpec((tile, HEAD_DIM), lambda h: (0, h))
    table = whole((tile, HEAD_DIM))
    return pl.pallas_call(
        functools.partial(rot_kernel, sizes),
        grid=(heads,),
        in_specs=[smem(), smem(), whole((8, HEAD_DIM)), half, half, half],
        out_specs=[half, kv_spec(tile), table, table, smem()],
        out_shape=[
            jax.ShapeDtypeStruct((tile, width), BF16),
            jax.ShapeDtypeStruct((2, tile, width), BF16),
            jax.ShapeDtypeStruct((tile, HEAD_DIM), F32),
            jax.ShapeDtypeStruct((tile, HEAD_DIM), F32),
            jax.ShapeDtypeStruct((24,), jnp.int32),
        ],
        compiler_params=params("arbitrary"),
        name="rot",
    )(reach, tile_map.T, jnp.asarray(lane_freqs()), q_in, k_in, v_in)


def open_block(info, h, a, b):
    ok = (info[8 + 2 * h] >= abs(a)) & (info[9 + 2 * h] >= abs(b))
    if a:
        row = info[0] + a
        ok = ok & (row >= 0) & (row < info[2])
    if b:
        col = info[1] + b
        ok = ok & (col >= 0) & (col < info[3])
    return ok


def mask_column(mask):
    closed = jnp.where(mask[...] == 1, 0.0, NEG).astype(F32)
    return jnp.transpose(jnp.broadcast_to(closed, (8, closed.shape[1])))[:, 0:1]


def fwd_block(keys, values, extra, q, m, l, acc):
    s = dot_nt(keys, q[...]) * C1
    if extra is not None:
        s = s + extra
    m_old = m[0:1, :]
    m_new = jnp.maximum(m_old, jnp.max(s, axis=0, keepdims=True))
    p = jnp.exp2(s - m_new)
    alpha = jnp.exp2(m_old - m_new)
    m[0:1, :] = m_new
    l[0:1, :] = l[0:1, :] * alpha + jnp.sum(p, axis=0, keepdims=True)
    acc[...] = acc[...] * alpha + dot_tn(values, p.astype(BF16))


def fwd_own_kernel(q, own, tk, tv, mask, acc, m, l):
    m[...] = jnp.full(m.shape, NEG, F32)
    l[...] = jnp.zeros(l.shape, F32)
    acc[...] = jnp.zeros(acc.shape, F32)
    fwd_block(own[0], own[1], None, q, m, l, acc)
    fwd_block(tk[...], tv[...], mask_column(mask), q, m, l, acc)


def fwd_rows_kernel(info, q, up, down, acc_in, m_in, l_in, acc, m, l):
    h = pl.program_id(0)
    acc[...] = acc_in[...]
    m[...] = m_in[...]
    l[...] = l_in[...]
    for a, ref in ((-1, up), (1, down)):

        @pl.when(open_block(info, h, a, 0))
        def _(ref=ref):
            fwd_block(ref[0], ref[1], None, q, m, l, acc)


def kv_spec(tile):
    return pl.BlockSpec((2, tile, HEAD_DIM), lambda h: (0, 0, h))


def stack_spec(tile):
    return pl.BlockSpec((3, 2, tile, HEAD_DIM), lambda h: (0, 0, 0, h))


def half_spec(rows):
    return pl.BlockSpec((rows, HEAD_DIM), lambda h: (0, h))


def row_spec(rows, tile):
    return pl.BlockSpec((rows, tile), lambda h: (h, 0))


def fwd_own_call(q, own, text_keys, text_values, mask):
    tile, width = q.shape
    heads = width // HEAD_DIM
    txt = text_keys.shape[0]
    keys = tile + txt
    stats = jax.ShapeDtypeStruct((8 * heads, tile), F32)
    return pl.pallas_call(
        fwd_own_kernel,
        grid=(heads,),
        in_specs=[
            half_spec(tile),
            kv_spec(tile),
            half_spec(txt),
            half_spec(txt),
            whole((1, txt)),
        ],
        out_specs=[row_spec(HEAD_DIM, tile), row_spec(8, tile), row_spec(8, tile)],
        out_shape=[jax.ShapeDtypeStruct((width, tile), F32), stats, stats],
        compiler_params=params("arbitrary"),
        cost_estimate=pl.CostEstimate(
            flops=4 * tile * keys * width, bytes_accessed=4 * keys * width, transcendentals=0
        ),
        name="fwd_own",
    )(q, own, text_keys, text_values, mask)


def fwd_rows_call(info, q, up, down, acc, m, l):
    tile, width = q.shape
    state_specs = [row_spec(HEAD_DIM, tile), row_spec(8, tile), row_spec(8, tile)]
    keys = 2 * tile
    return pl.pallas_call(
        fwd_rows_kernel,
        grid=(width // HEAD_DIM,),
        in_specs=[smem(), half_spec(tile), kv_spec(tile), kv_spec(tile)] + state_specs,
        out_specs=state_specs,
        out_shape=[jax.ShapeDtypeStruct(x.shape, F32) for x in (acc, m, l)],
        compiler_params=params("arbitrary"),
        cost_estimate=pl.CostEstimate(
            flops=4 * tile * keys * width, bytes_accessed=4 * keys * width, transcendentals=0
        ),
        name="fwd_rows",
    )(info, q, up, down, acc, m, l)


def stack_kernel(up, own, down, out):
    out[0] = up[...]
    out[1] = own[...]
    out[2] = down[...]


def stack_call(up, own, down):
    tile, width = own.shape[1:]
    return pl.pallas_call(
        stack_kernel,
        grid=(width // HEAD_DIM,),
        in_specs=[kv_spec(tile)] * 3,
        out_specs=stack_spec(tile),
        out_shape=jax.ShapeDtypeStruct((3, 2, tile, width), BF16),
        compiler_params=params("arbitrary", limit=SMALL),
        name="stack",
    )(up, own, down)


def first_block(info, flip, ys, xs):
    return (ys - 1 - info[4] if flip else info[4]) * xs


def fetch(w, pieces, w_buf, p_buf, sems, slot, block):
    cols = p_buf.shape[2]
    at = pl.multiple_of(block * cols, 128)
    copies = [
        pltpu.make_async_copy(pieces, p_buf.at[slot], sems.at[2 * slot]),
        pltpu.make_async_copy(
            w.at[:, pl.ds(at, cols)], w_buf.at[slot], sems.at[2 * slot + 1]
        ),
    ]
    for copy in copies:
        copy.start()
    return copies


def proj_piece(gate, w_buf, p_buf, slot, block):
    cols = p_buf.shape[2]
    at = pl.multiple_of(block * cols, 128)
    scaled = (p_buf[slot].astype(F32) * gate[:, pl.ds(at, cols)]).astype(BF16)
    return dot_nt(w_buf[slot], scaled)


def proj_kernel(ys, xs, info, w, gate, pieces, out, w_buf, p_buf, sems):
    start = first_block(info, False, ys, xs)
    copies = [
        fetch(w, pieces.at[x], w_buf, p_buf, sems, x, start + x) for x in range(xs)
    ]
    acc = None
    for x in range(xs):
        for copy in copies[x]:
            copy.wait()
        part = proj_piece(gate, w_buf, p_buf, x, start + x)
        acc = part if acc is None else acc + part
    out[...] = acc


def proj_call(sizes, info, w, gate, pieces):
    ys, xs = sizes[3:]
    width = w.shape[0]
    _, tile, cols = pieces.shape
    vmem = pl.BlockSpec(memory_space=pltpu.VMEM)
    hbm = pl.BlockSpec(memory_space=pltpu.HBM)
    return pl.pallas_call(
        functools.partial(proj_kernel, ys, xs),
        in_specs=[smem(), hbm, vmem, hbm],
        out_specs=vmem,
        out_shape=jax.ShapeDtypeStruct((width, tile), F32),
        scratch_shapes=[
            pltpu.VMEM((xs, width, cols), BF16),
            pltpu.VMEM((xs, tile, cols), BF16),
            pltpu.SemaphoreType.DMA((2 * xs,)),
        ],
        compiler_params=params(),
        cost_estimate=pl.CostEstimate(
            flops=2 * tile * width * cols * xs,
            bytes_accessed=2 * (tile + width) * cols * xs,
            transcendentals=0,
        ),
        name="proj",
    )(info, w, gate, pieces)


def middle_kernel(ys, xs, *refs):
    info, w, near, far, left, right, gate, q, acc_proj, acc_in, m_in, l_in = refs[:12]
    dot_out, ot_out, lse_out, delta_out, gate_out = refs[12:17]
    w_buf, p_buf, side_buf, sems, kv_sems, acc, m, l, gates = refs[17:]
    jobs = []
    kv_copies = []
    for flip, pieces in ((True, far), (False, near)):
        start = first_block(info, flip, ys, xs)
        for x in range(xs):
            slot = len(jobs)
            copies = fetch(w, pieces.at[x], w_buf, p_buf, sems, slot, start + x)
            jobs.append((slot, start + x, copies))
        if flip:
            for i, source in enumerate((left, right)):
                copy = pltpu.make_async_copy(source, side_buf.at[i], kv_sems.at[i])
                copy.start()
                kv_copies.append(copy)

    acc[...] = acc_in[...]
    m[...] = m_in[...]
    l[...] = l_in[...]
    total = acc_proj[...]
    for slot, block, copies in jobs[:xs]:
        for copy in copies:
            copy.wait()
        total = total + proj_piece(gate, w_buf, p_buf, slot, block)
    dot_out[...] = total.astype(BF16)

    for copy in kv_copies:
        copy.wait()
    width, tile = acc.shape
    for h in range(width // HEAD_DIM):
        lanes = slice(h * HEAD_DIM, (h + 1) * HEAD_DIM)
        stats = slice(8 * h, 8 * h + 8)
        state = (q.at[:, lanes], m.at[stats], l.at[stats], acc.at[lanes])
        for b, i in ((-1, 0), (1, 1)):
            for a in (-1, 0, 1):

                @pl.when(open_block(info, h, a, b))
                def _(i=i, a=a, lanes=lanes, state=state):
                    fwd_block(
                        side_buf[i, a + 1, 0, :, lanes],
                        side_buf[i, a + 1, 1, :, lanes],
                        None,
                        *state,
                    )

        norm = l[8 * h : 8 * h + 1, :]
        ot = (acc[lanes, :] * (1.0 / norm)).astype(BF16)
        ot_out[lanes, :] = ot
        lse = m[8 * h : 8 * h + 1, :] + jnp.log2(norm)
        lse_out[stats, :] = jnp.broadcast_to(lse, (8, tile))
        delta = jnp.sum(
            ot.astype(F32) * dot_out[lanes, :].astype(F32), axis=0, keepdims=True
        )
        delta_out[stats, :] = jnp.broadcast_to(delta, (8, tile))

    count = p_buf.shape[2] // 128
    for n, (slot, block, copies) in enumerate(jobs):
        if n >= xs:
            for copy in copies:
                copy.wait()
        terms = dot_nn(ot_out[...], p_buf[slot]) * w_buf[slot].astype(F32)
        row = jnp.sum(terms, axis=0, keepdims=True)
        for i in range(count):
            gates[pl.ds(block * count + i, 1), :] = row[:, i * 128 : (i + 1) * 128]
    for i in range(gate_out.shape[0]):
        gate_out[i] = gates[...]


def middle_call(sizes, info, w, near, far, left, right, gate, q, acc_proj, partial):
    ys, xs = sizes[3:]
    tile, width = q.shape
    heads = width // HEAD_DIM
    cols = near.shape[2]
    rows = w.shape[1] // 128
    vmem = pl.BlockSpec(memory_space=pltpu.VMEM)
    hbm = pl.BlockSpec(memory_space=pltpu.HBM)
    stats = jax.ShapeDtypeStruct((8 * heads, tile), F32)
    plane = jax.ShapeDtypeStruct((width, tile), BF16)
    keys = 6 * tile
    return pl.pallas_call(
        functools.partial(middle_kernel, ys, xs),
        in_specs=[smem()] + [hbm] * 5 + [vmem] * 6,
        out_specs=[vmem] * 5,
        out_shape=[
            plane,
            plane,
            stats,
            stats,
            jax.ShapeDtypeStruct((sizes[2] * ys * xs, rows, 128), F32),
        ],
        scratch_shapes=[
            pltpu.VMEM((ys * xs, width, cols), BF16),
            pltpu.VMEM((ys * xs, tile, cols), BF16),
            pltpu.VMEM((2, 3, 2, tile, width), BF16),
            pltpu.SemaphoreType.DMA((2 * ys * xs,)),
            pltpu.SemaphoreType.DMA((2,)),
            pltpu.VMEM((width, tile), F32),
            pltpu.VMEM((8 * heads, tile), F32),
            pltpu.VMEM((8 * heads, tile), F32),
            pltpu.VMEM((rows, 128), F32),
        ],
        compiler_params=params(),
        cost_estimate=pl.CostEstimate(
            flops=4 * tile * keys * width, bytes_accessed=8 * keys * width, transcendentals=0
        ),
        name="middle",
    )(info, w, near, far, left, right, gate, q, acc_proj, *partial)


def bwd_math(keys, values, q, dot, lse, delta, dq, extra):
    s = dot_nt(keys, q[...]) * C1
    if extra is not None:
        s = s + extra
    p = jnp.exp2(s - lse[0:1, :])
    dp = dot_nn(values, dot[...])
    ds = (p * (dp - delta[0:1, :])).astype(BF16)
    dv = dot_nt(p.astype(BF16), dot[...])
    dk = dot_nn(ds, q[...]) * SCALE
    dq[...] += dot_tn(keys, ds)
    return dk, dv


def bwd_block(info, h, a, b, block, out, q, dot, lse, delta, dq):
    def run():
        dk, dv = bwd_math(block[0], block[1], q, dot, lse, delta, dq, None)
        out[0] = dk.astype(out.dtype)
        out[1] = dv.astype(out.dtype)

    if (a, b) == (0, 0):
        run()
    else:
        ok = open_block(info, h, a, b)
        pl.when(ok)(run)

        @pl.when(jnp.logical_not(ok))
        def _():
            out[...] = jnp.zeros(out.shape, out.dtype)


def bwd_side_kernel(
    info, q, dot, lse, delta, tk, tv, mask, left, right, left_out, right_out, keep, give, dq_out
):
    h = pl.program_id(0)
    dq_out[...] = jnp.zeros(dq_out.shape, F32)
    dk, dv = bwd_math(tk[...], tv[...], q, dot, lse, delta, dq_out, mask_column(mask))
    first = info[5] == 0
    keep[...] = jnp.where(first, dk, dv)
    give[...] = jnp.where(first, dv, dk).astype(BF16)
    for b, ref, out in ((-1, left, left_out), (1, right, right_out)):
        for a in (-1, 0, 1):
            bwd_block(
                info, h, a, b, ref.at[a + 1], out.at[a + 1], q, dot, lse, delta, dq_out
            )


def bwd_near_kernel(
    info, q, dot, lse, delta, dq_in, cos, sin, up, own, down, left, right, *refs
):
    up_out, own_out, down_out, gq_out, dq = refs
    h = pl.program_id(0)
    dq[...] = dq_in[...]
    for a, ref, out in ((-1, up, up_out), (1, down, down_out), (0, own, own_out)):
        came = [left[a + 1, i].astype(F32) + right[a + 1, i].astype(F32) for i in (0, 1)]

        def run(ref=ref, out=out, came=came):
            dk, dv = bwd_math(ref[0], ref[1], q, dot, lse, delta, dq, None)
            out[0] = (dk + came[0]).astype(out.dtype)
            out[1] = (dv + came[1]).astype(out.dtype)

        if a == 0:
            run()
            continue
        ok = open_block(info, h, a, 0)
        pl.when(ok)(run)

        @pl.when(jnp.logical_not(ok))
        def _(out=out, came=came):
            out[0] = came[0].astype(out.dtype)
            out[1] = came[1].astype(out.dtype)

    x = jnp.transpose(dq[...]) * SCALE
    lane = lax.broadcasted_iota(jnp.int32, x.shape, 1)
    gq_out[...] = (x * cos[...] - partner(x, lane) * sin[...]).astype(BF16)


def bwd_specs(tile):
    return [
        smem(),
        pl.BlockSpec((tile, HEAD_DIM), lambda h: (0, h)),
        pl.BlockSpec((HEAD_DIM, tile), lambda h: (h, 0)),
        pl.BlockSpec((8, tile), lambda h: (h, 0)),
        pl.BlockSpec((8, tile), lambda h: (h, 0)),
    ]


def bwd_cost(tile, keys, width):
    return pl.CostEstimate(
        flops=10 * tile * keys * width, bytes_accessed=8 * keys * width, transcendentals=0
    )


def bwd_side_call(common, text_keys, text_values, mask, left, right):
    info, q, dot, lse, delta = common
    tile, width = q.shape
    txt = text_keys.shape[0]
    stack = jax.ShapeDtypeStruct((3, 2, tile, width), BF16)
    return pl.pallas_call(
        bwd_side_kernel,
        grid=(width // HEAD_DIM,),
        in_specs=bwd_specs(tile)
        + [half_spec(txt), half_spec(txt), whole((1, txt))]
        + [stack_spec(tile)] * 2,
        out_specs=[stack_spec(tile)] * 2
        + [half_spec(txt), half_spec(txt), row_spec(HEAD_DIM, tile)],
        out_shape=[
            stack,
            stack,
            jax.ShapeDtypeStruct((txt, width), F32),
            jax.ShapeDtypeStruct((txt, width), BF16),
            jax.ShapeDtypeStruct((width, tile), F32),
        ],
        compiler_params=params("arbitrary"),
        cost_estimate=bwd_cost(tile, 6 * tile + txt, width),
        name="bwd_side",
    )(info, q, dot, lse, delta, text_keys, text_values, mask, left, right)


def bwd_near_call(common, dq, cos, sin, up, own, down, left, right):
    info, q, dot, lse, delta = common
    tile, width = q.shape
    table = whole((tile, HEAD_DIM))
    return pl.pallas_call(
        bwd_near_kernel,
        grid=(width // HEAD_DIM,),
        in_specs=bwd_specs(tile)
        + [row_spec(HEAD_DIM, tile), table, table]
        + [kv_spec(tile)] * 3
        + [stack_spec(tile)] * 2,
        out_specs=[kv_spec(tile)] * 3 + [half_spec(tile)],
        out_shape=[
            jax.ShapeDtypeStruct((2, tile, width), BF16),
            jax.ShapeDtypeStruct((2, tile, width), F32),
            jax.ShapeDtypeStruct((2, tile, width), BF16),
            jax.ShapeDtypeStruct((tile, width), BF16),
        ],
        scratch_shapes=[pltpu.VMEM((HEAD_DIM, tile), F32)],
        compiler_params=params("arbitrary"),
        cost_estimate=bwd_cost(tile, 3 * tile, width),
        name="bwd_near",
    )(info, q, dot, lse, delta, dq, cos, sin, up, own, down, left, right)


def finish_kernel(own, up, down, cos, sin, gk_out, gv_out):
    total = own[...] + up[...].astype(F32) + down[...].astype(F32)
    x = total[0]
    lane = lax.broadcasted_iota(jnp.int32, x.shape, 1)
    gk_out[...] = (x * cos[...] - partner(x, lane) * sin[...]).astype(BF16)
    gv_out[...] = total[1].astype(BF16)


def finish_call(own, up, down, cos, sin):
    tile, width = own.shape[1:]
    table = whole((tile, HEAD_DIM))
    shape = jax.ShapeDtypeStruct((tile, width), BF16)
    return pl.pallas_call(
        finish_kernel,
        grid=(width // HEAD_DIM,),
        in_specs=[kv_spec(tile)] * 3 + [table, table],
        out_specs=[half_spec(tile)] * 2,
        out_shape=[shape, shape],
        compiler_params=params("arbitrary"),
        name="finish",
    )(own, up, down, cos, sin)


def split_pair(values):
    hi = values.astype(BF16)
    return hi, (values - hi.astype(F32)).astype(BF16)


def pack_kernel(keep, got, gate, out):
    groups, rows, _ = out.shape
    width = keep.shape[1]
    text = (keep[...] + got[...].astype(F32)).astype(BF16)
    out[:, :, :width] = text.reshape(groups, rows, width)
    out[:, :, width:] = jnp.zeros((groups, rows, 128), BF16)
    hi, lo = split_pair(jnp.sum(gate[...], axis=0))
    for i in range(gate.shape[1]):
        out[i, 0:1, width:] = hi[i : i + 1, :]
        out[i, 1:2, width:] = lo[i : i + 1, :]


def pack_call(keep, got, gate, groups):
    txt, width = keep.shape
    return pl.pallas_call(
        pack_kernel,
        in_specs=[pl.BlockSpec(memory_space=pltpu.VMEM)] * 3,
        out_specs=pl.BlockSpec(memory_space=pltpu.VMEM),
        out_shape=jax.ShapeDtypeStruct((groups, txt // groups, width + 128), BF16),
        compiler_params=params(limit=SMALL),
        name="pack",
    )(keep, got, gate)


def chunk_sum_kernel(width, got, out):
    total = jnp.sum(got[...].astype(F32), axis=0)
    text = total[:, :width].astype(BF16)
    hi, lo = split_pair(total[0:1, width:] + total[1:2, width:])
    row = lax.broadcasted_iota(jnp.int32, (total.shape[0], 128), 0)
    side = jnp.where(
        row == 0, hi.astype(F32), jnp.where(row == 1, lo.astype(F32), 0.0)
    ).astype(BF16)
    groups = out.shape[0]
    out[:, :, :width] = jnp.broadcast_to(text[None], (groups, *text.shape))
    out[:, :, width:] = jnp.broadcast_to(side[None], (groups, *side.shape))


def chunk_sum_call(got, width):
    return pl.pallas_call(
        functools.partial(chunk_sum_kernel, width),
        in_specs=[pl.BlockSpec(memory_space=pltpu.VMEM)],
        out_specs=pl.BlockSpec(memory_space=pltpu.VMEM),
        out_shape=jax.ShapeDtypeStruct(got.shape, BF16),
        compiler_params=params(limit=SMALL),
        name="chunk_sum",
    )(got)


def unpack_kernel(got, text_out, gate_out):
    groups, rows, _ = got.shape
    width = text_out.shape[1]
    text_out[...] = got[:, :, :width].reshape(groups * rows, width)
    for i in range(gate_out.shape[0]):
        pair = got[i, :, width:].astype(F32)
        gate_out[i : i + 1, :] = pair[0:1, :] + pair[1:2, :]


def unpack_call(got, width, gate_rows):
    groups, rows, _ = got.shape
    vmem = pl.BlockSpec(memory_space=pltpu.VMEM)
    return pl.pallas_call(
        unpack_kernel,
        in_specs=[vmem],
        out_specs=[vmem, vmem],
        out_shape=[
            jax.ShapeDtypeStruct((groups * rows, width), BF16),
            jax.ShapeDtypeStruct((gate_rows, 128), F32),
        ],
        compiler_params=params(limit=SMALL),
        name="unpack",
    )(got)


def choose_kernel(info, own, other, keys_out, values_out):
    first = info[5] == 0
    keys_out[...] = jnp.where(first, own[...], other[...])
    values_out[...] = jnp.where(first, other[...], own[...])


def choose_call(info, own, other):
    vmem = pl.BlockSpec(memory_space=pltpu.VMEM)
    shape = jax.ShapeDtypeStruct(own.shape, BF16)
    return pl.pallas_call(
        choose_kernel,
        in_specs=[smem(), vmem, vmem],
        out_specs=[vmem, vmem],
        out_shape=[shape, shape],
        compiler_params=params(limit=SMALL),
        name="choose",
    )(info, own, other)


def shift(array, axis, by, wrap=False):
    length = lax.axis_size(axis)
    pairs = [(i, (i + by) % length) for i in range(length) if wrap or 0 <= i + by < length]
    return lax.ppermute(array, axis, pairs)


def swap(array, axis, bit):
    length = lax.axis_size(axis)
    return lax.ppermute(array, axis, [(i, i ^ bit) for i in range(length)])


def spread(array, axis):
    copies = jnp.broadcast_to(array[None], (lax.axis_size(axis), *array.shape))
    return lax.all_to_all(copies, axis, 0, 0, tiled=True)


def on_device(
    query_in,
    key_in,
    value_in,
    text_keys,
    text_values,
    text_mask,
    window_reach,
    tile_map,
    out_weight,
    gate_scale,
    grad_out,
):
    _, width = query_in.shape
    sizes = tuple(lax.axis_size(axis) for axis in (*SEQ, *HEAD))
    mask = text_mask.reshape(1, -1)
    gate = gate_scale.reshape(1, -1)

    g_y = swap(grad_out, "yhi", 1)
    g_x = spread(grad_out, "x")

    q, kv, cos, sin, info = rotate_call(
        sizes, window_reach, tile_map, query_in, key_in, value_in
    )

    partial = fwd_own_call(q, kv, text_keys, text_values, mask)

    kv_up, kv_down = shift(kv, "z", 1), shift(kv, "z", -1)
    gy_x = spread(g_y, "x")
    stack = stack_call(kv_up, kv, kv_down)
    kv_left, kv_right = shift(stack, COL, 1), shift(stack, COL, -1)

    acc = proj_call(sizes, info, out_weight, gate, g_x)
    partial = fwd_rows_call(info, q, kv_up, kv_down, *partial)
    dot, _, lse, delta, gate_terms = middle_call(
        sizes,
        info,
        out_weight,
        g_x,
        gy_x,
        kv_left,
        kv_right,
        gate,
        q,
        acc,
        partial,
    )
    gate_terms = lax.all_to_all(gate_terms, ("core", *HEAD), 0, 0, tiled=True)

    common = (info, q, dot, lse, delta)
    left, right, keep, give, dq = bwd_side_call(
        common, text_keys, text_values, mask, kv_left, kv_right
    )
    taken = swap(give, "core", 1)
    back_left = shift(left, COL, -1)
    back_right = shift(right, COL, 1)
    packed = pack_call(keep, taken, gate_terms, lax.axis_size(CHIPS))
    got = lax.all_to_all(packed, CHIPS, 0, 0, tiled=True)
    up, own, down, grad_query = bwd_near_call(
        common, dq, cos, sin, kv_up, kv, kv_down, back_left, back_right
    )
    up = shift(up, "z", -1)
    down = shift(down, "z", 1)

    chunk = chunk_sum_call(got, width)
    summed = lax.all_to_all(chunk, CHIPS, 0, 0, tiled=True)
    own_text, grad_gate = unpack_call(summed, width, out_weight.shape[1] // 128)
    other_text = swap(own_text, "core", 1)
    grad_key, grad_value = finish_call(own, up, down, cos, sin)
    grad_text_keys, grad_text_values = choose_call(info, own_text, other_text)
    return (
        grad_query,
        grad_key,
        grad_value,
        grad_text_keys,
        grad_text_values,
        grad_gate.reshape(-1),
    )


def solution(mesh):
    fine = Mesh(mesh.devices.reshape(SIZES), (*SEQ, *HEAD))
    head = P(SEQ, HEAD)
    placed = (
        head,
        head,
        head,
        P(None, HEAD),
        P(None, HEAD),
        P(),
        P(HEAD, None),
        P(),
        P(HEAD, None),
        P(),
        head,
    )

    return jax.shard_map(
        on_device,
        mesh=fine,
        in_specs=placed,
        out_specs=(head, head, head, P(None, HEAD), P(None, HEAD), P()),
        check_vma=False,
    )


SIZES = (8, 4, 2, 2, 4)
```
